256 devices in a mesh: section: 4 (over y), ctx: 64 (over z, x, core).
Axes of the slice: x: 4, y: 4, z: 8, core: 2. Of those that a mesh axis runs over, the one named last changes fastest.
Arguments:
- incoming: bfloat16 [4, 8192, 4096], P('section', 'ctx'), may hold values from -6 to 6
- layer_input: bfloat16 [4, 8192, 4096], P('section', 'ctx'), may hold values from -6 to 6
- pre_gate: bfloat16 [4, 8192, 4096], P('section', 'ctx'), may hold values from -6 to 6
- mid_gate: bfloat16 [4, 8192, 4096], P('section', 'ctx'), may hold values from -6 to 6
- long_gate: bfloat16 [4, 8192, 4096], P('section', 'ctx'), may hold values from -6 to 6
- out_gate: bfloat16 [4, 8192, 4096], P('section', 'ctx'), may hold values from -6 to 6
- long_filter: bfloat16 [4, 4096, 8192], P('section', 'ctx'), may hold values from -0.0625 to 0.0625
- mid_filter: bfloat16 [4, 128, 4096], P('section'), may hold values from -0.5 to 0.5
Outputs:
- input_grad: bfloat16 [4, 8192, 4096], P('section', 'ctx')
- long_grad: bfloat16 [4, 4096, 8192], P('section', 'ctx')
- mid_grad: bfloat16 [4, 128, 4096], P('section', None, 'ctx')
The draws below stay inside these ranges and needn't reach their ends.
All inputs are finite; a program needn't handle non-finite values.
Results may differ from the reference program's by a relative error of at most 0.008.
Values may be sent and summed in bfloat16 or wider, within the bound.
A program may use at most 192 MiB of HBM per device.

```python
import math
import jax
import jax.numpy as jnp
from jax import lax

D = 4096
KM = 128
SECTIONS = 4
SEQ = 8192


def block_scale(key, shape, cuts, low, high):
    def one(dim, blocks):
        draws = jax.random.uniform(jax.random.fold_in(jax.random.fold_in(key, 6), dim), (blocks,), jnp.float32, low / len(cuts), high / len(cuts))
        return jnp.repeat(jnp.exp(draws), shape[dim] // blocks).reshape((-1,) + (1,) * (len(shape) - dim - 1))

    level = one(*cuts[0])
    for cut in cuts[1:]:
        level = level * one(*cut)
    return level


def centred(stream_key, extent, deviation, reach, split=(), kind=jnp.bfloat16):
    loudness = block_scale(stream_key, extent, split, -0.22, 0.18) if split else 1.0
    array = jax.random.normal(stream_key, extent, jnp.float32) * deviation * loudness
    return jnp.minimum(jnp.maximum(array, -reach), reach).astype(kind)


def setup_inputs(seed: int = 0) -> dict:
    key_list = jax.random.split(jax.random.key(seed), 9)
    incoming = centred(key_list[0], (SECTIONS, SEQ, D), 1.0, 6.0, ((0, 4), (1, 64)))
    layer_input = centred(key_list[1], (SECTIONS, SEQ, D), 1.0, 6.0, ((0, 4), (1, 64)))
    pre_gate = centred(key_list[2], (SECTIONS, SEQ, D), 1.0, 6.0, ((0, 4), (1, 64)))
    mid_gate = centred(key_list[3], (SECTIONS, SEQ, D), 1.0, 6.0, ((0, 4), (1, 64)))
    long_gate = centred(key_list[4], (SECTIONS, SEQ, D), 1.0, 6.0, ((0, 4), (1, 64)))
    out_gate = centred(key_list[5], (SECTIONS, SEQ, D), 1.0, 6.0, ((0, 4), (1, 64)))
    long_filter = centred(key_list[6], (SECTIONS, D, SEQ), SEQ ** -0.5, 0.0625, ((0, 4), (1, 64)))
    mid_filter = centred(key_list[7], (SECTIONS, KM, D), KM ** -0.5, 0.5, ((0, 4),))
    return dict(incoming=incoming, layer_input=layer_input, pre_gate=pre_gate, mid_gate=mid_gate, long_gate=long_gate, out_gate=out_gate, long_filter=long_filter, mid_filter=mid_filter)


def causal_mix(signal, filter_taps):
    padded = jnp.concatenate([jnp.zeros((KM - 1, D), signal.dtype), signal], 0)

    def add_tap(index, total):
        window = lax.dynamic_slice_in_dim(padded, KM - 1 - index, SEQ, 0)
        return total + filter_taps[index].astype(jnp.float32) * window.astype(jnp.float32)

    return lax.fori_loop(0, KM, add_tap, jnp.zeros((SEQ, D), jnp.float32))


def anticausal_mix(signal, filter_taps):
    padded = jnp.concatenate([signal, jnp.zeros((KM - 1, D), signal.dtype)], 0)

    def add_tap(index, total):
        window = lax.dynamic_slice_in_dim(padded, index, SEQ, 0)
        return total + filter_taps[index].astype(jnp.float32) * window.astype(jnp.float32)

    return lax.fori_loop(0, KM, add_tap, jnp.zeros((SEQ, D), jnp.float32))


def tap_sums(grad_b, mixed_in):
    padded = jnp.concatenate([jnp.zeros((KM - 1, D), mixed_in.dtype), mixed_in], 0)

    def one_tap(index):
        window = lax.dynamic_slice_in_dim(padded, KM - 1 - index, SEQ, 0)
        return jnp.sum(grad_b.astype(jnp.float32) * window.astype(jnp.float32), axis=0)

    return lax.map(one_tap, jnp.arange(KM, dtype=jnp.int32))


def long_pass(grad_z, long_in, filt):
    block = math.gcd(D, 256)
    length = 2 * SEQ
    shaped_z = grad_z.T.reshape(D // block, block, SEQ)
    shaped_w = long_in.T.reshape(D // block, block, SEQ)
    shaped_h = filt.reshape(D // block, block, SEQ)

    def one_block(pieces):
        piece_z, piece_w, piece_h = pieces
        spec_z = jnp.fft.rfft(piece_z.astype(jnp.float32), n=length, axis=-1)
        spec_w = jnp.fft.rfft(piece_w.astype(jnp.float32), n=length, axis=-1)
        spec_h = jnp.fft.rfft(piece_h.astype(jnp.float32), n=length, axis=-1)
        lag_grad = jnp.fft.irfft(spec_z * jnp.conj(spec_w), n=length, axis=-1)[:, :SEQ]
        input_part = jnp.fft.irfft(spec_z * jnp.conj(spec_h), n=length, axis=-1)[:, :SEQ]
        return lag_grad, input_part

    lag_grad, input_part = lax.map(one_block, (shaped_z, shaped_w, shaped_h))
    return lag_grad.reshape(D, SEQ), input_part.reshape(D, SEQ).T


def reference(incoming, layer_input, pre_gate, mid_gate, long_gate, out_gate, long_filter, mid_filter):
    beta = (2.0 * SECTIONS) ** -0.5
    scale = float(SEQ) ** -0.5
    input_list, long_list, mid_list = [], [], []
    for section_index in range(SECTIONS):
        adjoint = incoming[(section_index + 1) % SECTIONS].astype(jnp.float32)
        inputs = layer_input[section_index].astype(jnp.float32)
        gate_pre = pre_gate[section_index].astype(jnp.float32)
        gate_mid = mid_gate[section_index].astype(jnp.float32)
        gate_long = long_gate[section_index].astype(jnp.float32)
        gate_out = out_gate[section_index].astype(jnp.float32)
        filter_taps = mid_filter[section_index]
        mixed_in = (inputs * gate_pre).astype(jnp.bfloat16)
        branch = causal_mix(mixed_in, filter_taps)
        resid = inputs + beta * branch * gate_mid
        long_in = (resid * gate_long).astype(jnp.bfloat16)
        grad_z = (beta * adjoint * gate_out).astype(jnp.bfloat16)
        lag_grad, input_part = long_pass(grad_z, long_in, long_filter[section_index])
        long_list.append((lag_grad * scale).astype(jnp.bfloat16))
        grad_w = input_part.astype(jnp.bfloat16)
        grad_u = adjoint + grad_w.astype(jnp.float32) * gate_long
        grad_b = (beta * grad_u * gate_mid).astype(jnp.bfloat16)
        grad_act = anticausal_mix(grad_b, filter_taps)
        input_list.append((grad_u + grad_act * gate_pre).astype(jnp.bfloat16))
        mid_list.append((tap_sums(grad_b, mixed_in) * scale).astype(jnp.bfloat16))
    return (jnp.stack(input_list, 0), jnp.stack(long_list, 0), jnp.stack(mid_list, 0))
```

```python
import math

import jax
import jax.numpy as jnp
from jax import lax
from jax.sharding import PartitionSpec as P


def passed_along(value, axis, steps):
    count = lax.axis_size(axis)
    pairs = [(source, (source + steps) % count) for source in range(count)]
    return lax.ppermute(value, axis, pairs)


def shifted(array, axis, by):
    devices = lax.axis_size(axis)
    pairs = [(i, i + by) for i in range(devices) if 0 <= i + by < devices]
    return lax.ppermute(array, axis, pairs)


def unit_roots(rows, cols, period):
    row_ids = jnp.arange(rows, dtype=jnp.int32)[:, None]
    col_ids = jnp.arange(cols, dtype=jnp.int32)[None, :]
    angle = (row_ids * col_ids % period).astype(jnp.float32) * (-2.0 * math.pi / period)
    return (jnp.cos(angle), jnp.sin(angle))


def contract(form, left, right):
    return jnp.einsum(
        form, left, right, precision=lax.Precision.HIGH, preferred_element_type=jnp.float32
    )


def to_spectrum(parts, factor_a, factor_b):
    channels = parts.shape[0]
    inputs_count = parts.shape[1]
    half = factor_a // 2
    period = factor_a * factor_b
    fa_cos, fa_sin = unit_roots(factor_a, half, factor_a)
    first_table = jnp.stack([jnp.stack([fa_cos, -fa_sin]), jnp.stack([fa_sin, fa_cos])])[
        :, :inputs_count
    ]
    tw_cos, tw_sin = unit_roots(factor_a, factor_b, period)
    fb_cos, fb_sin = unit_roots(factor_b, factor_b, factor_b)
    second_table = jnp.stack([jnp.stack([fb_cos, fb_sin]), jnp.stack([-fb_sin, fb_cos])])
    shaped = parts.reshape(channels, inputs_count, half, factor_b)
    first = contract("qrca,nrab->nqcb", first_table, shaped)
    first_re = first[:, 0]
    first_im = first[:, 1]
    turned = jnp.stack(
        [first_re * tw_cos - first_im * tw_sin, first_re * tw_sin + first_im * tw_cos], 1
    )
    return contract("nqcb,qpbd->npcd", turned, second_table)


def from_spectrum(spectrum, factor_a, factor_b, scale):
    channels = spectrum.shape[0]
    half = factor_a // 2
    period = factor_a * factor_b
    fb_cos, fb_sin = unit_roots(factor_b, factor_b, factor_b)
    back_table = jnp.stack([jnp.stack([fb_cos, -fb_sin]), jnp.stack([fb_sin, fb_cos])])
    tw_cos, tw_sin = unit_roots(factor_a, factor_b, period)
    fa_cos, fa_sin = unit_roots(half, factor_a, factor_a)
    last_table = jnp.stack(
        [
            jnp.stack([fa_cos, fa_sin]) * (scale / period),
            jnp.stack([-fa_sin, fa_cos]) * (1.0 / period),
        ]
    )
    middle = contract("npcd,pqdb->nqcb", spectrum, back_table)
    middle_re = middle[:, 0]
    middle_im = middle[:, 1]
    turned = jnp.stack(
        [middle_re * tw_cos + middle_im * tw_sin, middle_im * tw_cos - middle_re * tw_sin], 1
    )
    result = contract("rqac,nqcb->nrab", last_table, turned)
    length = half * factor_b
    return (result[:, 0].reshape(channels, length), result[:, 1].reshape(channels, length))


def depthwise(extended, kernel):
    result = lax.conv_general_dilated(
        extended[None],
        kernel[:, None, :],
        (1,),
        "VALID",
        dimension_numbers=("NWC", "WIO", "NWC"),
        feature_group_count=extended.shape[1],
        preferred_element_type=jnp.float32,
    )
    return result[0]


def per_device(
    incoming, layer_input, pre_gate, mid_gate, long_gate, out_gate, long_filter, mid_filter
):
    sections = lax.axis_size("section")
    beta = (2.0 * sections) ** (-0.5)
    adjoint = passed_along(incoming[0], "section", -1).astype(jnp.float32)
    inputs = layer_input[0].astype(jnp.float32)
    tokens = inputs.shape[0]
    gate_pre = pre_gate[0].astype(jnp.float32)
    gate_mid = mid_gate[0].astype(jnp.float32)
    gate_long = long_gate[0].astype(jnp.float32)
    gate_out = out_gate[0].astype(jnp.float32)
    filter_taps = mid_filter[0]
    reach = filter_taps.shape[0] - 1
    seq_len = tokens * lax.axis_size("ctx")
    scale = float(seq_len) ** (-0.5)
    mixed_in = (inputs * gate_pre).astype(jnp.bfloat16)
    earlier = shifted(mixed_in[tokens - reach :], "ctx", 1)
    extended = jnp.concatenate([earlier, mixed_in], 0)
    branch = depthwise(extended, filter_taps[::-1])
    resid = inputs + beta * branch * gate_mid
    long_in = (resid * gate_long).astype(jnp.bfloat16)
    grad_z = (beta * adjoint * gate_out).astype(jnp.bfloat16)
    channel_z, channel_w = (
        lax.all_to_all(grad_z.T, "ctx", split_axis=0, concat_axis=1, tiled=True),
        lax.all_to_all(long_in.T, "ctx", split_axis=0, concat_axis=1, tiled=True),
    )
    factor_b = math.gcd(seq_len, 128)
    factor_a = 2 * seq_len // factor_b
    zspec = to_spectrum(channel_z[:, None], factor_a, factor_b)
    zspec_re = zspec[:, 0]
    zspec_im = zspec[:, 1]
    pair = to_spectrum(jnp.stack([channel_w, -long_filter[0]], 1), factor_a, factor_b)
    pair_re = pair[:, 0]
    pair_im = pair[:, 1]
    joint_re = zspec_re * pair_re + zspec_im * pair_im
    joint_im = zspec_im * pair_re - zspec_re * pair_im
    lag_grad, input_part = from_spectrum(
        jnp.stack([joint_re, joint_im], 1), factor_a, factor_b, scale
    )
    long_grad = lag_grad.astype(jnp.bfloat16)[None]
    returned = lax.all_to_all(
        input_part.astype(jnp.bfloat16), "ctx", split_axis=1, concat_axis=0, tiled=True
    ).T
    grad_u = adjoint + returned.astype(jnp.float32) * gate_long
    grad_b = (beta * grad_u * gate_mid).astype(jnp.bfloat16)
    later = shifted(grad_b[:reach], "ctx", -1)
    grad_act = depthwise(jnp.concatenate([grad_b, later], 0), filter_taps)
    input_grad = (grad_u + grad_act * gate_pre).astype(jnp.bfloat16)[None]
    tap_part = depthwise(extended, grad_b)[::-1]
    own_taps = lax.psum_scatter(tap_part, "ctx", scatter_dimension=1, tiled=True)
    mid_grad = (own_taps * scale).astype(jnp.bfloat16)[None]
    return (input_grad, long_grad, mid_grad)


def solution(mesh):
    placed = (
        P("section", "ctx", None),
        P("section", "ctx", None),
        P("section", "ctx", None),
        P("section", "ctx", None),
        P("section", "ctx", None),
        P("section", "ctx", None),
        P("section", "ctx", None),
        P("section", None, None),
    )
    return jax.shard_map(
        per_device,
        mesh=mesh,
        in_specs=placed,
        out_specs=(P("section", "ctx", None), P("section", "ctx", None), P("section", None, "ctx")),
        check_vma=False,
    )
```

```python
import functools
import math

import jax
import jax.numpy as jnp
from jax import lax
from jax.experimental import pallas as pl
from jax.experimental.pallas import tpu as pltpu
from jax.sharding import PartitionSpec as P

MESH_IDS = pl.DeviceIdType.MESH


def tap_exchange_kernel(n, scale, x_ref, o_ref, recv, send_sems, recv_sems):
    me = lax.axis_index("ctx")
    sec = lax.axis_index("section")
    barrier = pltpu.get_barrier_semaphore()

    def greet(k, carry):
        peer = lax.rem(me + k, n)
        pl.semaphore_signal(barrier, inc=1, device_id=(sec, peer), device_id_type=MESH_IDS)
        return carry

    lax.fori_loop(1, n, greet, 0)
    pl.semaphore_wait(barrier, n - 1)

    def copy_to(peer):
        return pltpu.make_async_remote_copy(
            src_ref=x_ref.at[peer],
            dst_ref=recv.at[me],
            send_sem=send_sems.at[peer],
            recv_sem=recv_sems.at[me],
            device_id=(sec, peer),
            device_id_type=MESH_IDS,
        )

    def start(k, carry):
        copy_to(lax.rem(me + k, n)).start()
        return carry

    lax.fori_loop(1, n, start, 0)
    recv[me] = x_ref[me]

    def wait_from(k, carry):
        src = lax.rem(me + n - k, n)
        pltpu.make_async_remote_copy(
            src_ref=x_ref.at[src],
            dst_ref=recv.at[src],
            send_sem=send_sems.at[src],
            recv_sem=recv_sems.at[src],
            device_id=(sec, src),
            device_id_type=MESH_IDS,
        ).wait_recv()
        copy_to(lax.rem(me + k, n)).wait_send()
        return carry

    lax.fori_loop(1, n, wait_from, 0)
    o_ref[...] = (jnp.sum(recv[...], axis=0) * scale).astype(o_ref.dtype)


def tap_exchange(parts, scale):
    n, taps, width = parts.shape
    return pl.pallas_call(
        functools.partial(tap_exchange_kernel, n, scale),
        out_shape=jax.ShapeDtypeStruct((taps, width), jnp.bfloat16),
        in_specs=[pl.BlockSpec(memory_space=pltpu.VMEM)],
        out_specs=pl.BlockSpec(memory_space=pltpu.VMEM),
        scratch_shapes=[
            pltpu.VMEM((n, taps, width), jnp.float32),
            pltpu.SemaphoreType.DMA((n,)),
            pltpu.SemaphoreType.DMA((n,)),
        ],
        compiler_params=pltpu.CompilerParams(collective_id=0, has_side_effects=True),
    )(parts)


def passed_along(value, axis, steps):
    count = lax.axis_size(axis)
    pairs = [(source, (source + steps) % count) for source in range(count)]
    return lax.ppermute(value, axis, pairs)


def shifted(array, axis, by):
    devices = lax.axis_size(axis)
    pairs = [(i, i + by) for i in range(devices) if 0 <= i + by < devices]
    return lax.ppermute(array, axis, pairs)


def unit_roots(rows, cols, period):
    row_ids = jnp.arange(rows, dtype=jnp.int32)[:, None]
    col_ids = jnp.arange(cols, dtype=jnp.int32)[None, :]
    angle = (row_ids * col_ids % period).astype(jnp.float32) * (-2.0 * math.pi / period)
    return (jnp.cos(angle), jnp.sin(angle))


def contract(form, left, right):
    return jnp.einsum(
        form, left, right, precision=lax.Precision.HIGH, preferred_element_type=jnp.float32
    )


def to_spectrum(parts, factor_a, factor_b):
    channels = parts.shape[0]
    inputs_count = parts.shape[1]
    half = factor_a // 2
    period = factor_a * factor_b
    fa_cos, fa_sin = unit_roots(factor_a, half, factor_a)
    first_table = jnp.stack([jnp.stack([fa_cos, -fa_sin]), jnp.stack([fa_sin, fa_cos])])[
        :, :inputs_count
    ]
    tw_cos, tw_sin = unit_roots(factor_a, factor_b, period)
    fb_cos, fb_sin = unit_roots(factor_b, factor_b, factor_b)
    second_table = jnp.stack([jnp.stack([fb_cos, fb_sin]), jnp.stack([-fb_sin, fb_cos])])
    shaped = parts.reshape(channels, inputs_count, half, factor_b)
    first = contract("qrca,nrab->nqcb", first_table, shaped)
    first_re = first[:, 0]
    first_im = first[:, 1]
    turned = jnp.stack(
        [first_re * tw_cos - first_im * tw_sin, first_re * tw_sin + first_im * tw_cos], 1
    )
    return contract("nqcb,qpbd->npcd", turned, second_table)


def from_spectrum(spectrum, factor_a, factor_b, scale):
    channels = spectrum.shape[0]
    half = factor_a // 2
    period = factor_a * factor_b
    fb_cos, fb_sin = unit_roots(factor_b, factor_b, factor_b)
    back_table = jnp.stack([jnp.stack([fb_cos, -fb_sin]), jnp.stack([fb_sin, fb_cos])])
    tw_cos, tw_sin = unit_roots(factor_a, factor_b, period)
    fa_cos, fa_sin = unit_roots(half, factor_a, factor_a)
    last_table = jnp.stack(
        [
            jnp.stack([fa_cos, fa_sin]) * (scale / period),
            jnp.stack([-fa_sin, fa_cos]) * (1.0 / period),
        ]
    )
    middle = contract("npcd,pqdb->nqcb", spectrum, back_table)
    middle_re = middle[:, 0]
    middle_im = middle[:, 1]
    turned = jnp.stack(
        [middle_re * tw_cos + middle_im * tw_sin, middle_im * tw_cos - middle_re * tw_sin], 1
    )
    result = contract("rqac,nqcb->nrab", last_table, turned)
    length = half * factor_b
    return (result[:, 0].reshape(channels, length), result[:, 1].reshape(channels, length))


def depthwise(extended, kernel):
    result = lax.conv_general_dilated(
        extended[None],
        kernel[:, None, :],
        (1,),
        "VALID",
        dimension_numbers=("NWC", "WIO", "NWC"),
        feature_group_count=extended.shape[1],
        preferred_element_type=jnp.float32,
    )
    return result[0]


def per_device(
    incoming, layer_input, pre_gate, mid_gate, long_gate, out_gate, long_filter, mid_filter
):
    sections = lax.axis_size("section")
    beta = (2.0 * sections) ** (-0.5)
    adjoint = passed_along(incoming[0], "section", -1).astype(jnp.float32)
    inputs = layer_input[0].astype(jnp.float32)
    tokens = inputs.shape[0]
    gate_pre = pre_gate[0].astype(jnp.float32)
    gate_mid = mid_gate[0].astype(jnp.float32)
    gate_long = long_gate[0].astype(jnp.float32)
    gate_out = out_gate[0].astype(jnp.float32)
    filter_taps = mid_filter[0]
    reach = filter_taps.shape[0] - 1
    seq_len = tokens * lax.axis_size("ctx")
    scale = float(seq_len) ** (-0.5)
    mixed_in = (inputs * gate_pre).astype(jnp.bfloat16)
    earlier = shifted(mixed_in[tokens - reach :], "ctx", 1)
    extended = jnp.concatenate([earlier, mixed_in], 0)
    branch = depthwise(extended, filter_taps[::-1])
    resid = inputs + beta * branch * gate_mid
    long_in = (resid * gate_long).astype(jnp.bfloat16)
    grad_z = (beta * adjoint * gate_out).astype(jnp.bfloat16)
    channel_z, channel_w = (
        lax.all_to_all(grad_z.T, "ctx", split_axis=0, concat_axis=1, tiled=True),
        lax.all_to_all(long_in.T, "ctx", split_axis=0, concat_axis=1, tiled=True),
    )
    factor_b = math.gcd(seq_len, 128)
    factor_a = 2 * seq_len // factor_b
    zspec = to_spectrum(channel_z[:, None], factor_a, factor_b)
    zspec_re = zspec[:, 0]
    zspec_im = zspec[:, 1]
    pair = to_spectrum(jnp.stack([channel_w, -long_filter[0]], 1), factor_a, factor_b)
    pair_re = pair[:, 0]
    pair_im = pair[:, 1]
    joint_re = zspec_re * pair_re + zspec_im * pair_im
    joint_im = zspec_im * pair_re - zspec_re * pair_im
    lag_grad, input_part = from_spectrum(
        jnp.stack([joint_re, joint_im], 1), factor_a, factor_b, scale
    )
    long_grad = lag_grad.astype(jnp.bfloat16)[None]
    returned = lax.all_to_all(
        input_part.astype(jnp.bfloat16), "ctx", split_axis=1, concat_axis=0, tiled=True
    ).T
    grad_u = adjoint + returned.astype(jnp.float32) * gate_long
    grad_b = (beta * grad_u * gate_mid).astype(jnp.bfloat16)
    later = shifted(grad_b[:reach], "ctx", -1)
    grad_act = depthwise(jnp.concatenate([grad_b, later], 0), filter_taps)
    input_grad = (grad_u + grad_act * gate_pre).astype(jnp.bfloat16)[None]
    tap_part = depthwise(extended, grad_b)[::-1]
    devices = lax.axis_size("ctx")
    columns = tap_part.shape[1] // devices
    parts = tap_part.reshape(tap_part.shape[0], devices, columns).transpose(1, 0, 2)
    mid_grad = tap_exchange(parts, scale)[None]
    return (input_grad, long_grad, mid_grad)


def solution(mesh):
    placed = (
        P("section", "ctx", None),
        P("section", "ctx", None),
        P("section", "ctx", None),
        P("section", "ctx", None),
        P("section", "ctx", None),
        P("section", "ctx", None),
        P("section", "ctx", None),
        P("section", None, None),
    )
    return jax.shard_map(
        per_device,
        mesh=mesh,
        in_specs=placed,
        out_specs=(P("section", "ctx", None), P("section", "ctx", None), P("section", None, "ctx")),
        check_vma=False,
    )
```

```python
import functools
import math

import jax
import jax.numpy as jnp
from jax import lax
from jax.experimental import pallas as pl
from jax.experimental.pallas import tpu as pltpu
from jax.sharding import PartitionSpec as P

MESH_IDS = pl.DeviceIdType.MESH


def tap_exchange_kernel(nz, nx, nc, scale, x_ref, o_ref, r1, s1, r2, s2, r3, sems):
    me = lax.axis_index("ctx")
    sec = lax.axis_index("section")
    core = me % nc
    xi = (me // nc) % nx
    zi = me // (nc * nx)

    def device(z, x, c):
        return (sec, (z * nx + x) * nc + c)

    peers = [device(zi, xi, 1 - core)]
    peers += [device(zi, (xi + k) % nx, core) for k in range(1, nx)]
    peers += [device((zi + k) % nz, xi, core) for k in range(1, nz)]
    barrier = pltpu.get_barrier_semaphore()
    for peer in peers:
        pl.semaphore_signal(barrier, inc=1, device_id=peer, device_id_type=MESH_IDS)
    pl.semaphore_wait(barrier, len(peers))

    def send(src, dst, peer, out_slot, in_slot):
        return pltpu.make_async_remote_copy(
            src_ref=src,
            dst_ref=dst,
            send_sem=sems.at[0, out_slot],
            recv_sem=sems.at[1, in_slot],
            device_id=peer,
            device_id_type=MESH_IDS,
        )

    first = send(x_ref.at[1 - core], r1, peers[0], 0, 0)
    first.start()
    first.wait()
    s1[...] = x_ref[core] + r1[...]

    second = []
    for k in range(1, nx):
        target = (xi + k) % nx
        copy = send(s1.at[target], r2.at[xi], device(zi, target, core), 1 + target, 1 + xi)
        copy.start()
        second.append(copy)
    for k in range(1, nx):
        source = (xi + nx - k) % nx
        send(s1.at[source], r2.at[source], device(zi, source, core), 1 + source, 1 + source).wait_recv()
    for copy in second:
        copy.wait_send()
    r2[xi] = s1[xi]
    s2[...] = jnp.sum(r2[...], axis=0)

    third = []
    for k in range(1, nz):
        target = (zi + k) % nz
        copy = send(s2.at[target], r3.at[zi], device(target, xi, core), 1 + nx + target, 1 + nx + zi)
        copy.start()
        third.append(copy)
    for k in range(1, nz):
        source = (zi + nz - k) % nz
        send(s2.at[source], r3.at[source], device(source, xi, core), 1 + nx + source, 1 + nx + source).wait_recv()
    for copy in third:
        copy.wait_send()
    r3[zi] = s2[zi]
    o_ref[...] = (jnp.sum(r3[...], axis=0) * scale).astype(o_ref.dtype)


def tap_exchange(parts, scale):
    nc, nx, nz, taps, width = parts.shape
    return pl.pallas_call(
        functools.partial(tap_exchange_kernel, nz, nx, nc, scale),
        out_shape=jax.ShapeDtypeStruct((taps, width), jnp.bfloat16),
        in_specs=[pl.BlockSpec(memory_space=pltpu.VMEM)],
        out_specs=pl.BlockSpec(memory_space=pltpu.VMEM),
        scratch_shapes=[
            pltpu.VMEM((nx, nz, taps, width), jnp.float32),
            pltpu.VMEM((nx, nz, taps, width), jnp.float32),
            pltpu.VMEM((nx, nz, taps, width), jnp.float32),
            pltpu.VMEM((nz, taps, width), jnp.float32),
            pltpu.VMEM((nz, taps, width), jnp.float32),
            pltpu.SemaphoreType.DMA((2, 1 + nx + nz)),
        ],
        compiler_params=pltpu.CompilerParams(collective_id=0, has_side_effects=True),
    )(parts)


def passed_along(value, axis, steps):
    count = lax.axis_size(axis)
    pairs = [(source, (source + steps) % count) for source in range(count)]
    return lax.ppermute(value, axis, pairs)


def shifted(array, axis, by):
    devices = lax.axis_size(axis)
    pairs = [(i, i + by) for i in range(devices) if 0 <= i + by < devices]
    return lax.ppermute(array, axis, pairs)


def unit_roots(rows, cols, period):
    row_ids = jnp.arange(rows, dtype=jnp.int32)[:, None]
    col_ids = jnp.arange(cols, dtype=jnp.int32)[None, :]
    angle = (row_ids * col_ids % period).astype(jnp.float32) * (-2.0 * math.pi / period)
    return (jnp.cos(angle), jnp.sin(angle))


def contract(form, left, right):
    return jnp.einsum(
        form, left, right, precision=lax.Precision.HIGH, preferred_element_type=jnp.float32
    )


def to_spectrum(parts, factor_a, factor_b):
    channels = parts.shape[0]
    inputs_count = parts.shape[1]
    half = factor_a // 2
    period = factor_a * factor_b
    fa_cos, fa_sin = unit_roots(factor_a, half, factor_a)
    first_table = jnp.stack([jnp.stack([fa_cos, -fa_sin]), jnp.stack([fa_sin, fa_cos])])[
        :, :inputs_count
    ]
    tw_cos, tw_sin = unit_roots(factor_a, factor_b, period)
    fb_cos, fb_sin = unit_roots(factor_b, factor_b, factor_b)
    second_table = jnp.stack([jnp.stack([fb_cos, fb_sin]), jnp.stack([-fb_sin, fb_cos])])
    shaped = parts.reshape(channels, inputs_count, half, factor_b)
    first = contract("qrca,nrab->nqcb", first_table, shaped)
    first_re = first[:, 0]
    first_im = first[:, 1]
    turned = jnp.stack(
        [first_re * tw_cos - first_im * tw_sin, first_re * tw_sin + first_im * tw_cos], 1
    )
    return contract("nqcb,qpbd->npcd", turned, second_table)


def from_spectrum(spectrum, factor_a, factor_b, scale):
    channels = spectrum.shape[0]
    half = factor_a // 2
    period = factor_a * factor_b
    fb_cos, fb_sin = unit_roots(factor_b, factor_b, factor_b)
    back_table = jnp.stack([jnp.stack([fb_cos, -fb_sin]), jnp.stack([fb_sin, fb_cos])])
    tw_cos, tw_sin = unit_roots(factor_a, factor_b, period)
    fa_cos, fa_sin = unit_roots(half, factor_a, factor_a)
    last_table = jnp.stack(
        [
            jnp.stack([fa_cos, fa_sin]) * (scale / period),
            jnp.stack([-fa_sin, fa_cos]) * (1.0 / period),
        ]
    )
    middle = contract("npcd,pqdb->nqcb", spectrum, back_table)
    middle_re = middle[:, 0]
    middle_im = middle[:, 1]
    turned = jnp.stack(
        [middle_re * tw_cos + middle_im * tw_sin, middle_im * tw_cos - middle_re * tw_sin], 1
    )
    result = contract("rqac,nqcb->nrab", last_table, turned)
    length = half * factor_b
    return (result[:, 0].reshape(channels, length), result[:, 1].reshape(channels, length))


def depthwise(extended, kernel):
    result = lax.conv_general_dilated(
        extended[None],
        kernel[:, None, :],
        (1,),
        "VALID",
        dimension_numbers=("NWC", "WIO", "NWC"),
        feature_group_count=extended.shape[1],
        preferred_element_type=jnp.float32,
    )
    return result[0]


def per_device(
    incoming, layer_input, pre_gate, mid_gate, long_gate, out_gate, long_filter, mid_filter
):
    sections = lax.axis_size("section")
    beta = (2.0 * sections) ** (-0.5)
    adjoint = passed_along(incoming[0], "section", -1).astype(jnp.float32)
    inputs = layer_input[0].astype(jnp.float32)
    tokens = inputs.shape[0]
    gate_pre = pre_gate[0].astype(jnp.float32)
    gate_mid = mid_gate[0].astype(jnp.float32)
    gate_long = long_gate[0].astype(jnp.float32)
    gate_out = out_gate[0].astype(jnp.float32)
    filter_taps = mid_filter[0]
    reach = filter_taps.shape[0] - 1
    seq_len = tokens * lax.axis_size("ctx")
    scale = float(seq_len) ** (-0.5)
    mixed_in = (inputs * gate_pre).astype(jnp.bfloat16)
    earlier = shifted(mixed_in[tokens - reach :], "ctx", 1)
    extended = jnp.concatenate([earlier, mixed_in], 0)
    branch = depthwise(extended, filter_taps[::-1])
    resid = inputs + beta * branch * gate_mid
    long_in = (resid * gate_long).astype(jnp.bfloat16)
    grad_z = (beta * adjoint * gate_out).astype(jnp.bfloat16)
    channel_z, channel_w = (
        lax.all_to_all(grad_z.T, "ctx", split_axis=0, concat_axis=1, tiled=True),
        lax.all_to_all(long_in.T, "ctx", split_axis=0, concat_axis=1, tiled=True),
    )
    factor_b = math.gcd(seq_len, 128)
    factor_a = 2 * seq_len // factor_b
    zspec = to_spectrum(channel_z[:, None], factor_a, factor_b)
    zspec_re = zspec[:, 0]
    zspec_im = zspec[:, 1]
    pair = to_spectrum(jnp.stack([channel_w, -long_filter[0]], 1), factor_a, factor_b)
    pair_re = pair[:, 0]
    pair_im = pair[:, 1]
    joint_re = zspec_re * pair_re + zspec_im * pair_im
    joint_im = zspec_im * pair_re - zspec_re * pair_im
    lag_grad, input_part = from_spectrum(
        jnp.stack([joint_re, joint_im], 1), factor_a, factor_b, scale
    )
    long_grad = lag_grad.astype(jnp.bfloat16)[None]
    returned = lax.all_to_all(
        input_part.astype(jnp.bfloat16), "ctx", split_axis=1, concat_axis=0, tiled=True
    ).T
    grad_u = adjoint + returned.astype(jnp.float32) * gate_long
    grad_b = (beta * grad_u * gate_mid).astype(jnp.bfloat16)
    later = shifted(grad_b[:reach], "ctx", -1)
    grad_act = depthwise(jnp.concatenate([grad_b, later], 0), filter_taps)
    input_grad = (grad_u + grad_act * gate_pre).astype(jnp.bfloat16)[None]
    tap_part = depthwise(extended, grad_b)[::-1]
    devices = lax.axis_size("ctx")
    columns = tap_part.shape[1] // devices
    chip_cores, chips_x = 2, 4
    chips_z = devices // (chip_cores * chips_x)
    parts = tap_part.reshape(tap_part.shape[0], chips_z, chips_x, chip_cores, columns)
    parts = parts.transpose(3, 2, 1, 0, 4)
    mid_grad = tap_exchange(parts, scale)[None]
    return (input_grad, long_grad, mid_grad)


def solution(mesh):
    placed = (
        P("section", "ctx", None),
        P("section", "ctx", None),
        P("section", "ctx", None),
        P("section", "ctx", None),
        P("section", "ctx", None),
        P("section", "ctx", None),
        P("section", "ctx", None),
        P("section", None, None),
    )
    return jax.shard_map(
        per_device,
        mesh=mesh,
        in_specs=placed,
        out_specs=(P("section", "ctx", None), P("section", "ctx", None), P("section", None, "ctx")),
        check_vma=False,
    )
```

```python
import functools
import math

import jax
import jax.numpy as jnp
from jax import lax
from jax.experimental import pallas as pl
from jax.experimental.pallas import tpu as pltpu
from jax.sharding import PartitionSpec as P

MESH_IDS = pl.DeviceIdType.MESH


def tap_exchange_kernel(nz, nx, nc, scale, x_ref, o_ref, r1, s1, r2, s2, r3, sems):
    me = lax.axis_index("ctx")
    sec = lax.axis_index("section")
    core = me % nc
    xi = (me // nc) % nx
    zi = me // (nc * nx)

    def device(z, x, c):
        return (sec, (z * nx + x) * nc + c)

    peers = [device(zi, xi, 1 - core)]
    peers += [device(zi, (xi + k) % nx, core) for k in range(1, nx)]
    peers += [device((zi + k) % nz, xi, core) for k in range(1, nz)]
    barrier = pltpu.get_barrier_semaphore()
    for peer in peers:
        pl.semaphore_signal(barrier, inc=1, device_id=peer, device_id_type=MESH_IDS)
    pl.semaphore_wait(barrier, len(peers))

    def send(src, dst, peer, out_slot, in_slot):
        return pltpu.make_async_remote_copy(
            src_ref=src,
            dst_ref=dst,
            send_sem=sems.at[0, out_slot],
            recv_sem=sems.at[1, in_slot],
            device_id=peer,
            device_id_type=MESH_IDS,
        )

    first = send(x_ref.at[1 - core], r1, peers[0], 0, 0)
    first.start()
    first.wait()
    s1[...] = x_ref[core] + r1[...]

    second = []
    for k in range(1, nx):
        target = (xi + k) % nx
        copy = send(s1.at[target], r2.at[xi], device(zi, target, core), 1 + target, 1 + xi)
        copy.start()
        second.append(copy)
    for k in range(1, nx):
        source = (xi + nx - k) % nx
        send(s1.at[source], r2.at[source], device(zi, source, core), 1 + source, 1 + source).wait_recv()
    for copy in second:
        copy.wait_send()
    r2[xi] = s1[xi]
    s2[...] = jnp.sum(r2[...], axis=0)

    third = []
    for k in range(1, nz):
        target = (zi + k) % nz
        copy = send(s2.at[target], r3.at[zi], device(target, xi, core), 1 + nx + target, 1 + nx + zi)
        copy.start()
        third.append(copy)
    for k in range(1, nz):
        source = (zi + nz - k) % nz
        send(s2.at[source], r3.at[source], device(source, xi, core), 1 + nx + source, 1 + nx + source).wait_recv()
    for copy in third:
        copy.wait_send()
    r3[zi] = s2[zi]
    o_ref[...] = (jnp.sum(r3[...], axis=0) * scale).astype(o_ref.dtype)


def tap_exchange(parts, scale):
    nc, nx, nz, taps, width = parts.shape
    return pl.pallas_call(
        functools.partial(tap_exchange_kernel, nz, nx, nc, scale),
        out_shape=jax.ShapeDtypeStruct((taps, width), jnp.bfloat16),
        in_specs=[pl.BlockSpec(memory_space=pltpu.VMEM)],
        out_specs=pl.BlockSpec(memory_space=pltpu.VMEM),
        scratch_shapes=[
            pltpu.VMEM((nx, nz, taps, width), jnp.float32),
            pltpu.VMEM((nx, nz, taps, width), jnp.float32),
            pltpu.VMEM((nx, nz, taps, width), jnp.float32),
            pltpu.VMEM((nz, taps, width), jnp.float32),
            pltpu.VMEM((nz, taps, width), jnp.float32),
            pltpu.SemaphoreType.DMA((2, 1 + nx + nz)),
        ],
        compiler_params=pltpu.CompilerParams(collective_id=0, has_side_effects=True),
    )(parts)


def passed_along(value, axis, steps):
    count = lax.axis_size(axis)
    pairs = [(source, (source + steps) % count) for source in range(count)]
    return lax.ppermute(value, axis, pairs)


def shifted(array, axis, by):
    devices = lax.axis_size(axis)
    pairs = [(i, i + by) for i in range(devices) if 0 <= i + by < devices]
    return lax.ppermute(array, axis, pairs)


def unit_roots(rows, cols, period):
    row_ids = jnp.arange(rows, dtype=jnp.int32)[:, None]
    col_ids = jnp.arange(cols, dtype=jnp.int32)[None, :]
    angle = (row_ids * col_ids % period).astype(jnp.float32) * (-2.0 * math.pi / period)
    return (jnp.cos(angle), jnp.sin(angle))


def contract(form, left, right):
    return jnp.einsum(
        form, left, right, precision=lax.Precision.HIGH, preferred_element_type=jnp.float32
    )


def to_spectrum(parts, factor_a, factor_b):
    channels = parts.shape[0]
    inputs_count = parts.shape[1]
    half = factor_a // 2
    period = factor_a * factor_b
    fa_cos, fa_sin = unit_roots(factor_a, half, factor_a)
    first_table = jnp.stack([jnp.stack([fa_cos, -fa_sin]), jnp.stack([fa_sin, fa_cos])])[
        :, :inputs_count
    ]
    tw_cos, tw_sin = unit_roots(factor_a, factor_b, period)
    fb_cos, fb_sin = unit_roots(factor_b, factor_b, factor_b)
    second_table = jnp.stack([jnp.stack([fb_cos, fb_sin]), jnp.stack([-fb_sin, fb_cos])])
    shaped = parts.reshape(channels, inputs_count, half, factor_b)
    first = contract("qrca,nrab->nqcb", first_table, shaped)
    first_re = first[:, 0]
    first_im = first[:, 1]
    turned = jnp.stack(
        [first_re * tw_cos - first_im * tw_sin, first_re * tw_sin + first_im * tw_cos], 1
    )
    return contract("nqcb,qpbd->npcd", turned, second_table)


def from_spectrum(spectrum, factor_a, factor_b, scale):
    channels = spectrum.shape[0]
    half = factor_a // 2
    period = factor_a * factor_b
    fb_cos, fb_sin = unit_roots(factor_b, factor_b, factor_b)
    back_table = jnp.stack([jnp.stack([fb_cos, -fb_sin]), jnp.stack([fb_sin, fb_cos])])
    tw_cos, tw_sin = unit_roots(factor_a, factor_b, period)
    fa_cos, fa_sin = unit_roots(half, factor_a, factor_a)
    last_table = jnp.stack(
        [
            jnp.stack([fa_cos, fa_sin]) * (scale / period),
            jnp.stack([-fa_sin, fa_cos]) * (1.0 / period),
        ]
    )
    middle = contract("npcd,pqdb->nqcb", spectrum, back_table)
    middle_re = middle[:, 0]
    middle_im = middle[:, 1]
    turned = jnp.stack(
        [middle_re * tw_cos + middle_im * tw_sin, middle_im * tw_cos - middle_re * tw_sin], 1
    )
    result = contract("rqac,nqcb->nrab", last_table, turned)
    length = half * factor_b
    return (result[:, 0].reshape(channels, length), result[:, 1].reshape(channels, length))


def depthwise(extended, kernel):
    result = lax.conv_general_dilated(
        extended[None],
        kernel[:, None, :],
        (1,),
        "VALID",
        dimension_numbers=("NWC", "WIO", "NWC"),
        feature_group_count=extended.shape[1],
        preferred_element_type=jnp.float32,
    )
    return result[0]


def per_device(
    incoming, layer_input, pre_gate, mid_gate, long_gate, out_gate, long_filter, mid_filter
):
    sections = lax.axis_size("section")
    beta = (2.0 * sections) ** (-0.5)
    adjoint = passed_along(incoming[0], "section", -1).astype(jnp.float32)
    inputs = layer_input[0].astype(jnp.float32)
    tokens = inputs.shape[0]
    gate_pre = pre_gate[0].astype(jnp.float32)
    gate_mid = mid_gate[0].astype(jnp.float32)
    gate_long = long_gate[0].astype(jnp.float32)
    gate_out = out_gate[0].astype(jnp.float32)
    filter_taps = mid_filter[0]
    reach = filter_taps.shape[0] - 1
    seq_len = tokens * lax.axis_size("ctx")
    scale = float(seq_len) ** (-0.5)
    mixed_in = (inputs * gate_pre).astype(jnp.bfloat16)
    earlier = shifted(mixed_in[tokens - reach :], "ctx", 1)
    extended = jnp.concatenate([earlier, mixed_in], 0)
    branch = depthwise(extended, filter_taps[::-1])
    resid = inputs + beta * branch * gate_mid
    long_in = (resid * gate_long).astype(jnp.bfloat16)
    grad_z = (beta * adjoint * gate_out).astype(jnp.bfloat16)
    channel_z, channel_w = lax.all_to_all(
        jnp.stack([grad_z.T, long_in.T]), "ctx", split_axis=1, concat_axis=2, tiled=True
    )
    factor_b = math.gcd(seq_len, 128)
    factor_a = 2 * seq_len // factor_b
    zspec = to_spectrum(channel_z[:, None], factor_a, factor_b)
    zspec_re = zspec[:, 0]
    zspec_im = zspec[:, 1]
    pair = to_spectrum(jnp.stack([channel_w, -long_filter[0]], 1), factor_a, factor_b)
    pair_re = pair[:, 0]
    pair_im = pair[:, 1]
    joint_re = zspec_re * pair_re + zspec_im * pair_im
    joint_im = zspec_im * pair_re - zspec_re * pair_im
    lag_grad, input_part = from_spectrum(
        jnp.stack([joint_re, joint_im], 1), factor_a, factor_b, scale
    )
    long_grad = lag_grad.astype(jnp.bfloat16)[None]
    returned = lax.all_to_all(
        input_part.astype(jnp.bfloat16), "ctx", split_axis=1, concat_axis=0, tiled=True
    ).T
    grad_u = adjoint + returned.astype(jnp.float32) * gate_long
    grad_b = (beta * grad_u * gate_mid).astype(jnp.bfloat16)
    later = shifted(grad_b[:reach], "ctx", -1)
    grad_act = depthwise(jnp.concatenate([grad_b, later], 0), filter_taps)
    input_grad = (grad_u + grad_act * gate_pre).astype(jnp.bfloat16)[None]
    tap_part = depthwise(extended, grad_b)
    devices = lax.axis_size("ctx")
    columns = tap_part.shape[1] // devices
    chip_cores, chips_x = 2, 4
    chips_z = devices // (chip_cores * chips_x)
    parts = tap_part.reshape(tap_part.shape[0], chips_z, chips_x, chip_cores, columns)
    parts = parts.transpose(3, 2, 1, 0, 4).reshape(
        chip_cores, chips_x, chips_z, tap_part.shape[0] * columns // 128, 128
    )
    mid_grad = tap_exchange(parts, scale).reshape(tap_part.shape[0], columns)[::-1][None]
    return (input_grad, long_grad, mid_grad)


def solution(mesh):
    placed = (
        P("section", "ctx", None),
        P("section", "ctx", None),
        P("section", "ctx", None),
        P("section", "ctx", None),
        P("section", "ctx", None),
        P("section", "ctx", None),
        P("section", "ctx", None),
        P("section", None, None),
    )
    return jax.shard_map(
        per_device,
        mesh=mesh,
        in_specs=placed,
        out_specs=(P("section", "ctx", None), P("section", "ctx", None), P("section", None, "ctx")),
        check_vma=False,
    )
```

```python
import functools
import math

import jax
import jax.numpy as jnp
from jax import lax
from jax.experimental import pallas as pl
from jax.experimental.pallas import tpu as pltpu
from jax.sharding import PartitionSpec as P

MESH_IDS = pl.DeviceIdType.MESH


def tap_exchange_kernel(nz, nx, nc, scale, x_ref, o_ref, r1, s1, r2, s2, r3, sems):
    me = lax.axis_index("ctx")
    sec = lax.axis_index("section")
    core = me % nc
    xi = (me // nc) % nx
    zi = me // (nc * nx)

    def device(z, x, c):
        return (sec, (z * nx + x) * nc + c)

    peers = [device(zi, xi, 1 - core)]
    peers += [device(zi, (xi + k) % nx, core) for k in range(1, nx)]
    peers += [device((zi + k) % nz, xi, core) for k in range(1, nz)]
    barrier = pltpu.get_barrier_semaphore()
    for peer in peers:
        pl.semaphore_signal(barrier, inc=1, device_id=peer, device_id_type=MESH_IDS)
    pl.semaphore_wait(barrier, len(peers))

    def send(src, dst, peer, out_slot, in_slot):
        return pltpu.make_async_remote_copy(
            src_ref=src,
            dst_ref=dst,
            send_sem=sems.at[0, out_slot],
            recv_sem=sems.at[1, in_slot],
            device_id=peer,
            device_id_type=MESH_IDS,
        )

    first = send(x_ref.at[:, :, 1 - core], r1, peers[0], 0, 0)
    first.start()
    first.wait()
    s1[...] = x_ref[:, :, core] + r1[...]

    second = []
    for k in range(1, nx):
        target = (xi + k) % nx
        copy = send(s1.at[:, target], r2.at[xi], device(zi, target, core), 1 + target, 1 + xi)
        copy.start()
        second.append(copy)
    for k in range(1, nx):
        source = (xi + nx - k) % nx
        send(s1.at[:, source], r2.at[source], device(zi, source, core), 1 + source, 1 + source).wait_recv()
    for copy in second:
        copy.wait_send()
    r2[xi] = s1[:, xi]
    s2[...] = jnp.sum(r2[...], axis=0)

    third = []
    for k in range(1, nz):
        target = (zi + k) % nz
        copy = send(s2.at[target], r3.at[zi], device(target, xi, core), 1 + nx + target, 1 + nx + zi)
        copy.start()
        third.append(copy)
    for k in range(1, nz):
        source = (zi + nz - k) % nz
        send(s2.at[source], r3.at[source], device(source, xi, core), 1 + nx + source, 1 + nx + source).wait_recv()
    for copy in third:
        copy.wait_send()
    r3[zi] = s2[zi]
    o_ref[...] = (jnp.sum(r3[...], axis=0) * scale).astype(o_ref.dtype)


def tap_exchange(parts, scale):
    nz, nx, nc, taps, width = parts.shape
    return pl.pallas_call(
        functools.partial(tap_exchange_kernel, nz, nx, nc, scale),
        out_shape=jax.ShapeDtypeStruct((taps, width), jnp.bfloat16),
        in_specs=[pl.BlockSpec(memory_space=pltpu.VMEM)],
        out_specs=pl.BlockSpec(memory_space=pltpu.VMEM),
        scratch_shapes=[
            pltpu.VMEM((nz, nx, taps, width), jnp.float32),
            pltpu.VMEM((nz, nx, taps, width), jnp.float32),
            pltpu.VMEM((nx, nz, taps, width), jnp.float32),
            pltpu.VMEM((nz, taps, width), jnp.float32),
            pltpu.VMEM((nz, taps, width), jnp.float32),
            pltpu.SemaphoreType.DMA((2, 1 + nx + nz)),
        ],
        compiler_params=pltpu.CompilerParams(collective_id=0, has_side_effects=True),
    )(parts)


def passed_along(value, axis, steps):
    count = lax.axis_size(axis)
    pairs = [(source, (source + steps) % count) for source in range(count)]
    return lax.ppermute(value, axis, pairs)


def shifted(array, axis, by):
    devices = lax.axis_size(axis)
    pairs = [(i, i + by) for i in range(devices) if 0 <= i + by < devices]
    return lax.ppermute(array, axis, pairs)


def unit_roots(rows, cols, period):
    row_ids = jnp.arange(rows, dtype=jnp.int32)[:, None]
    col_ids = jnp.arange(cols, dtype=jnp.int32)[None, :]
    angle = (row_ids * col_ids % period).astype(jnp.float32) * (-2.0 * math.pi / period)
    return (jnp.cos(angle), jnp.sin(angle))


def contract(form, left, right):
    return jnp.einsum(
        form, left, right, precision=lax.Precision.HIGH, preferred_element_type=jnp.float32
    )


def to_spectrum(parts, factor_a, factor_b):
    channels = parts.shape[0]
    inputs_count = parts.shape[1]
    half = factor_a // 2
    period = factor_a * factor_b
    fa_cos, fa_sin = unit_roots(factor_a, half, factor_a)
    first_table = jnp.stack([jnp.stack([fa_cos, -fa_sin]), jnp.stack([fa_sin, fa_cos])])[
        :, :inputs_count
    ]
    tw_cos, tw_sin = unit_roots(factor_a, factor_b, period)
    fb_cos, fb_sin = unit_roots(factor_b, factor_b, factor_b)
    second_table = jnp.stack([jnp.stack([fb_cos, fb_sin]), jnp.stack([-fb_sin, fb_cos])])
    shaped = parts.reshape(channels, inputs_count, half, factor_b)
    first = contract("qrca,nrab->nqcb", first_table, shaped)
    first_re = first[:, 0]
    first_im = first[:, 1]
    turned = jnp.stack(
        [first_re * tw_cos - first_im * tw_sin, first_re * tw_sin + first_im * tw_cos], 1
    )
    return contract("nqcb,qpbd->npcd", turned, second_table)


def from_spectrum(spectrum, factor_a, factor_b, scale):
    channels = spectrum.shape[0]
    half = factor_a // 2
    period = factor_a * factor_b
    fb_cos, fb_sin = unit_roots(factor_b, factor_b, factor_b)
    back_table = jnp.stack([jnp.stack([fb_cos, -fb_sin]), jnp.stack([fb_sin, fb_cos])])
    tw_cos, tw_sin = unit_roots(factor_a, factor_b, period)
    fa_cos, fa_sin = unit_roots(half, factor_a, factor_a)
    last_table = jnp.stack(
        [
            jnp.stack([fa_cos, fa_sin]) * (scale / period),
            jnp.stack([-fa_sin, fa_cos]) * (1.0 / period),
        ]
    )
    middle = contract("npcd,pqdb->nqcb", spectrum, back_table)
    middle_re = middle[:, 0]
    middle_im = middle[:, 1]
    turned = jnp.stack(
        [middle_re * tw_cos + middle_im * tw_sin, middle_im * tw_cos - middle_re * tw_sin], 1
    )
    result = contract("rqac,nqcb->nrab", last_table, turned)
    length = half * factor_b
    return (result[:, 0].reshape(channels, length), result[:, 1].reshape(channels, length))


def depthwise(extended, kernel):
    result = lax.conv_general_dilated(
        extended[None],
        kernel[:, None, :],
        (1,),
        "VALID",
        dimension_numbers=("NWC", "WIO", "NWC"),
        feature_group_count=extended.shape[1],
        preferred_element_type=jnp.float32,
    )
    return result[0]


def per_device(
    incoming, layer_input, pre_gate, mid_gate, long_gate, out_gate, long_filter, mid_filter
):
    sections = lax.axis_size("section")
    beta = (2.0 * sections) ** (-0.5)
    adjoint = passed_along(incoming[0], "section", -1).astype(jnp.float32)
    inputs = layer_input[0].astype(jnp.float32)
    tokens = inputs.shape[0]
    gate_pre = pre_gate[0].astype(jnp.float32)
    gate_mid = mid_gate[0].astype(jnp.float32)
    gate_long = long_gate[0].astype(jnp.float32)
    gate_out = out_gate[0].astype(jnp.float32)
    filter_taps = mid_filter[0]
    reach = filter_taps.shape[0] - 1
    seq_len = tokens * lax.axis_size("ctx")
    scale = float(seq_len) ** (-0.5)
    mixed_in = (inputs * gate_pre).astype(jnp.bfloat16)
    earlier = shifted(mixed_in[tokens - reach :], "ctx", 1)
    extended = jnp.concatenate([earlier, mixed_in], 0)
    flip = jnp.eye(filter_taps.shape[0], dtype=filter_taps.dtype)[::-1]
    flipped_taps = jnp.dot(flip, filter_taps, preferred_element_type=jnp.float32)
    branch = depthwise(extended, flipped_taps.astype(filter_taps.dtype))
    resid = inputs + beta * branch * gate_mid
    long_in = (resid * gate_long).astype(jnp.bfloat16)
    grad_z = (beta * adjoint * gate_out).astype(jnp.bfloat16)
    channel_z, channel_w = lax.all_to_all(
        jnp.stack([grad_z.T, long_in.T]), "ctx", split_axis=1, concat_axis=2, tiled=True
    )
    factor_b = math.gcd(seq_len, 128)
    factor_a = 2 * seq_len // factor_b
    zspec = to_spectrum(channel_z[:, None], factor_a, factor_b)
    zspec_re = zspec[:, 0]
    zspec_im = zspec[:, 1]
    pair = to_spectrum(jnp.stack([channel_w, -long_filter[0]], 1), factor_a, factor_b)
    pair_re = pair[:, 0]
    pair_im = pair[:, 1]
    joint_re = zspec_re * pair_re + zspec_im * pair_im
    joint_im = zspec_im * pair_re - zspec_re * pair_im
    lag_grad, input_part = from_spectrum(
        jnp.stack([joint_re, joint_im], 1), factor_a, factor_b, scale
    )
    long_grad = lag_grad.astype(jnp.bfloat16)[None]
    returned = lax.all_to_all(
        input_part.astype(jnp.bfloat16), "ctx", split_axis=1, concat_axis=0, tiled=True
    ).T
    grad_u = adjoint + returned.astype(jnp.float32) * gate_long
    grad_b = (beta * grad_u * gate_mid).astype(jnp.bfloat16)
    later = shifted(grad_b[:reach], "ctx", -1)
    grad_act = depthwise(jnp.concatenate([grad_b, later], 0), filter_taps)
    input_grad = (grad_u + grad_act * gate_pre).astype(jnp.bfloat16)[None]
    tap_part = lax.conv_general_dilated(
        extended[None],
        grad_b[:, None, :],
        (1,),
        "VALID",
        dimension_numbers=("NWC", "WIO", "NCW"),
        feature_group_count=extended.shape[1],
        preferred_element_type=jnp.float32,
    )[0]
    devices = lax.axis_size("ctx")
    columns = tap_part.shape[0] // devices
    chip_cores, chips_x = 2, 4
    chips_z = devices // (chip_cores * chips_x)
    parts = tap_part.reshape(chips_z, chips_x, chip_cores, columns, tap_part.shape[1])
    mid_grad = tap_exchange(parts, scale).T[::-1][None]
    return (input_grad, long_grad, mid_grad)


def solution(mesh):
    placed = (
        P("section", "ctx", None),
        P("section", "ctx", None),
        P("section", "ctx", None),
        P("section", "ctx", None),
        P("section", "ctx", None),
        P("section", "ctx", None),
        P("section", "ctx", None),
        P("section", None, None),
    )
    return jax.shard_map(
        per_device,
        mesh=mesh,
        in_specs=placed,
        out_specs=(P("section", "ctx", None), P("section", "ctx", None), P("section", None, "ctx")),
        check_vma=False,
    )
```

```python
import functools
import math

import jax
import jax.numpy as jnp
from jax import lax
from jax.experimental import pallas as pl
from jax.experimental.pallas import tpu as pltpu
from jax.sharding import PartitionSpec as P

MESH_IDS = pl.DeviceIdType.MESH


def tap_exchange_kernel(nz, nx, nc, scale, x_ref, o_ref, r1, s1, r2, s2, r3, sems):
    me = lax.axis_index("ctx")
    sec = lax.axis_index("section")
    core = me % nc
    xi = (me // nc) % nx
    zi = me // (nc * nx)

    def device(z, x, c):
        return (sec, (z * nx + x) * nc + c)

    peers = [device(zi, xi, 1 - core)]
    peers += [device(zi, (xi + k) % nx, core) for k in range(1, nx)]
    peers += [device((zi + k) % nz, xi, core) for k in range(1, nz)]
    barrier = pltpu.get_barrier_semaphore()
    for peer in peers:
        pl.semaphore_signal(barrier, inc=1, device_id=peer, device_id_type=MESH_IDS)
    pl.semaphore_wait(barrier, len(peers))

    def send(src, dst, peer, out_slot, in_slot):
        return pltpu.make_async_remote_copy(
            src_ref=src,
            dst_ref=dst,
            send_sem=sems.at[0, out_slot],
            recv_sem=sems.at[1, in_slot],
            device_id=peer,
            device_id_type=MESH_IDS,
        )

    first = send(x_ref.at[:, :, 1 - core], r1, peers[0], 0, 0)
    first.start()
    first.wait()
    s1[...] = x_ref[:, :, core] + r1[...]

    second = []
    for k in range(1, nx):
        target = (xi + k) % nx
        copy = send(s1.at[:, target], r2.at[xi], device(zi, target, core), 1 + target, 1 + xi)
        copy.start()
        second.append(copy)
    for k in range(1, nx):
        source = (xi + nx - k) % nx
        send(s1.at[:, source], r2.at[source], device(zi, source, core), 1 + source, 1 + source).wait_recv()
    for copy in second:
        copy.wait_send()
    r2[xi] = s1[:, xi]
    s2[...] = jnp.sum(r2[...], axis=0)

    third = []
    for k in range(1, nz):
        target = (zi + k) % nz
        copy = send(s2.at[target], r3.at[zi], device(target, xi, core), 1 + nx + target, 1 + nx + zi)
        copy.start()
        third.append(copy)
    for k in range(1, nz):
        source = (zi + nz - k) % nz
        send(s2.at[source], r3.at[source], device(source, xi, core), 1 + nx + source, 1 + nx + source).wait_recv()
    for copy in third:
        copy.wait_send()
    r3[zi] = s2[zi]
    o_ref[...] = (jnp.sum(r3[...], axis=0) * scale).astype(o_ref.dtype)


def tap_exchange(parts, scale):
    nz, nx, nc, taps, width = parts.shape
    return pl.pallas_call(
        functools.partial(tap_exchange_kernel, nz, nx, nc, scale),
        out_shape=jax.ShapeDtypeStruct((taps, width), jnp.bfloat16),
        in_specs=[pl.BlockSpec(memory_space=pltpu.VMEM)],
        out_specs=pl.BlockSpec(memory_space=pltpu.VMEM),
        scratch_shapes=[
            pltpu.VMEM((nz, nx, taps, width), jnp.float32),
            pltpu.VMEM((nz, nx, taps, width), jnp.float32),
            pltpu.VMEM((nx, nz, taps, width), jnp.float32),
            pltpu.VMEM((nz, taps, width), jnp.float32),
            pltpu.VMEM((nz, taps, width), jnp.float32),
            pltpu.SemaphoreType.DMA((2, 1 + nx + nz)),
        ],
        compiler_params=pltpu.CompilerParams(collective_id=0, has_side_effects=True),
    )(parts)


def exchange_kernel(n, send_part, recv_part, x_ref, o_ref, local_sem, send_sems, recv_sems):
    me = lax.axis_index("ctx")
    sec = lax.axis_index("section")
    barrier = pltpu.get_barrier_semaphore()

    def greet(k, carry):
        peer = lax.rem(me + k, n)
        pl.semaphore_signal(barrier, inc=1, device_id=(sec, peer), device_id_type=MESH_IDS)
        return carry

    lax.fori_loop(1, n, greet, 0)
    pl.semaphore_wait(barrier, n - 1)

    def copy(peer, source):
        return pltpu.make_async_remote_copy(
            src_ref=send_part(x_ref, peer),
            dst_ref=recv_part(o_ref, source),
            send_sem=send_sems.at[peer],
            recv_sem=recv_sems.at[source],
            device_id=(sec, peer),
            device_id_type=MESH_IDS,
        )

    def start(k, carry):
        copy(lax.rem(me + k, n), me).start()
        return carry

    lax.fori_loop(1, n, start, 0)
    own = pltpu.make_async_copy(send_part(x_ref, me), recv_part(o_ref, me), local_sem)
    own.start()

    def finish(k, carry):
        copy(lax.rem(me + n - k, n), lax.rem(me + n - k, n)).wait_recv()
        copy(lax.rem(me + k, n), me).wait_send()
        return carry

    lax.fori_loop(1, n, finish, 0)
    own.wait()


def exchange(x, out_shape, send_part, recv_part, collective):
    n = lax.axis_size("ctx")
    return pl.pallas_call(
        functools.partial(exchange_kernel, n, send_part, recv_part),
        out_shape=jax.ShapeDtypeStruct(out_shape, x.dtype),
        in_specs=[pl.BlockSpec(memory_space=pltpu.VMEM)],
        out_specs=pl.BlockSpec(memory_space=pltpu.VMEM),
        scratch_shapes=[
            pltpu.SemaphoreType.DMA(()),
            pltpu.SemaphoreType.DMA((n,)),
            pltpu.SemaphoreType.DMA((n,)),
        ],
        compiler_params=pltpu.CompilerParams(collective_id=collective, has_side_effects=True),
    )(x)


def to_channels(x):
    n = lax.axis_size("ctx")
    count, channels, tokens = x.shape
    rows = channels // n

    def send_part(ref, peer):
        return ref.at[:, pl.ds(pl.multiple_of(peer * rows, rows), rows), :]

    def recv_part(ref, source):
        return ref.at[:, :, pl.ds(pl.multiple_of(source * tokens, tokens), tokens)]

    return exchange(x, (count, rows, tokens * n), send_part, recv_part, 1)


def to_positions(x):
    n = lax.axis_size("ctx")
    rows, length = x.shape
    tokens = length // n

    def send_part(ref, peer):
        return ref.at[:, pl.ds(pl.multiple_of(peer * tokens, tokens), tokens)]

    def recv_part(ref, source):
        return ref.at[pl.ds(pl.multiple_of(source * rows, rows), rows), :]

    return exchange(x, (rows * n, tokens), send_part, recv_part, 2)


def passed_along(value, axis, steps):
    count = lax.axis_size(axis)
    pairs = [(source, (source + steps) % count) for source in range(count)]
    return lax.ppermute(value, axis, pairs)


def shifted(array, axis, by):
    devices = lax.axis_size(axis)
    pairs = [(i, i + by) for i in range(devices) if 0 <= i + by < devices]
    return lax.ppermute(array, axis, pairs)


def unit_roots(rows, cols, period):
    row_ids = jnp.arange(rows, dtype=jnp.int32)[:, None]
    col_ids = jnp.arange(cols, dtype=jnp.int32)[None, :]
    angle = (row_ids * col_ids % period).astype(jnp.float32) * (-2.0 * math.pi / period)
    return (jnp.cos(angle), jnp.sin(angle))


def contract(form, left, right):
    return jnp.einsum(
        form, left, right, precision=lax.Precision.HIGH, preferred_element_type=jnp.float32
    )


def to_spectrum(parts, factor_a, factor_b):
    channels = parts.shape[0]
    inputs_count = parts.shape[1]
    half = factor_a // 2
    period = factor_a * factor_b
    fa_cos, fa_sin = unit_roots(factor_a, half, factor_a)
    first_table = jnp.stack([jnp.stack([fa_cos, -fa_sin]), jnp.stack([fa_sin, fa_cos])])[
        :, :inputs_count
    ]
    tw_cos, tw_sin = unit_roots(factor_a, factor_b, period)
    fb_cos, fb_sin = unit_roots(factor_b, factor_b, factor_b)
    second_table = jnp.stack([jnp.stack([fb_cos, fb_sin]), jnp.stack([-fb_sin, fb_cos])])
    shaped = parts.reshape(channels, inputs_count, half, factor_b)
    first = contract("qrca,nrab->nqcb", first_table, shaped)
    first_re = first[:, 0]
    first_im = first[:, 1]
    turned = jnp.stack(
        [first_re * tw_cos - first_im * tw_sin, first_re * tw_sin + first_im * tw_cos], 1
    )
    return contract("nqcb,qpbd->npcd", turned, second_table)


def from_spectrum(spectrum, factor_a, factor_b, scale):
    channels = spectrum.shape[0]
    half = factor_a // 2
    period = factor_a * factor_b
    fb_cos, fb_sin = unit_roots(factor_b, factor_b, factor_b)
    back_table = jnp.stack([jnp.stack([fb_cos, -fb_sin]), jnp.stack([fb_sin, fb_cos])])
    tw_cos, tw_sin = unit_roots(factor_a, factor_b, period)
    fa_cos, fa_sin = unit_roots(half, factor_a, factor_a)
    last_table = jnp.stack(
        [
            jnp.stack([fa_cos, fa_sin]) * (scale / period),
            jnp.stack([-fa_sin, fa_cos]) * (1.0 / period),
        ]
    )
    middle = contract("npcd,pqdb->nqcb", spectrum, back_table)
    middle_re = middle[:, 0]
    middle_im = middle[:, 1]
    turned = jnp.stack(
        [middle_re * tw_cos + middle_im * tw_sin, middle_im * tw_cos - middle_re * tw_sin], 1
    )
    result = contract("rqac,nqcb->nrab", last_table, turned)
    length = half * factor_b
    return (result[:, 0].reshape(channels, length), result[:, 1].reshape(channels, length))


def depthwise(extended, kernel):
    result = lax.conv_general_dilated(
        extended[None],
        kernel[:, None, :],
        (1,),
        "VALID",
        dimension_numbers=("NWC", "WIO", "NWC"),
        feature_group_count=extended.shape[1],
        preferred_element_type=jnp.float32,
    )
    return result[0]


def per_device(
    incoming, layer_input, pre_gate, mid_gate, long_gate, out_gate, long_filter, mid_filter
):
    sections = lax.axis_size("section")
    beta = (2.0 * sections) ** (-0.5)
    adjoint = passed_along(incoming[0], "section", -1).astype(jnp.float32)
    inputs = layer_input[0].astype(jnp.float32)
    tokens = inputs.shape[0]
    gate_pre = pre_gate[0].astype(jnp.float32)
    gate_mid = mid_gate[0].astype(jnp.float32)
    gate_long = long_gate[0].astype(jnp.float32)
    gate_out = out_gate[0].astype(jnp.float32)
    filter_taps = mid_filter[0]
    reach = filter_taps.shape[0] - 1
    seq_len = tokens * lax.axis_size("ctx")
    scale = float(seq_len) ** (-0.5)
    mixed_in = (inputs * gate_pre).astype(jnp.bfloat16)
    earlier = shifted(mixed_in[tokens - reach :], "ctx", 1)
    extended = jnp.concatenate([earlier, mixed_in], 0)
    flip = jnp.eye(filter_taps.shape[0], dtype=filter_taps.dtype)[::-1]
    flipped_taps = jnp.dot(flip, filter_taps, preferred_element_type=jnp.float32)
    branch = depthwise(extended, flipped_taps.astype(filter_taps.dtype))
    resid = inputs + beta * branch * gate_mid
    long_in = (resid * gate_long).astype(jnp.bfloat16)
    grad_z = (beta * adjoint * gate_out).astype(jnp.bfloat16)
    channel_z, channel_w = to_channels(jnp.stack([grad_z.T, long_in.T]))
    factor_b = math.gcd(seq_len, 128)
    factor_a = 2 * seq_len // factor_b
    zspec = to_spectrum(channel_z[:, None], factor_a, factor_b)
    zspec_re = zspec[:, 0]
    zspec_im = zspec[:, 1]
    pair = to_spectrum(jnp.stack([channel_w, -long_filter[0]], 1), factor_a, factor_b)
    pair_re = pair[:, 0]
    pair_im = pair[:, 1]
    joint_re = zspec_re * pair_re + zspec_im * pair_im
    joint_im = zspec_im * pair_re - zspec_re * pair_im
    lag_grad, input_part = from_spectrum(
        jnp.stack([joint_re, joint_im], 1), factor_a, factor_b, scale
    )
    long_grad = lag_grad.astype(jnp.bfloat16)[None]
    returned = to_positions(input_part.astype(jnp.bfloat16)).T
    grad_u = adjoint + returned.astype(jnp.float32) * gate_long
    grad_b = (beta * grad_u * gate_mid).astype(jnp.bfloat16)
    later = shifted(grad_b[:reach], "ctx", -1)
    grad_act = depthwise(jnp.concatenate([grad_b, later], 0), filter_taps)
    input_grad = (grad_u + grad_act * gate_pre).astype(jnp.bfloat16)[None]
    tap_part = lax.conv_general_dilated(
        extended[None],
        grad_b[:, None, :],
        (1,),
        "VALID",
        dimension_numbers=("NWC", "WIO", "NCW"),
        feature_group_count=extended.shape[1],
        preferred_element_type=jnp.float32,
    )[0]
    devices = lax.axis_size("ctx")
    columns = tap_part.shape[0] // devices
    chip_cores, chips_x = 2, 4
    chips_z = devices // (chip_cores * chips_x)
    parts = tap_part.reshape(chips_z, chips_x, chip_cores, columns, tap_part.shape[1])
    mid_grad = tap_exchange(parts, scale).T[::-1][None]
    return (input_grad, long_grad, mid_grad)


def solution(mesh):
    placed = (
        P("section", "ctx", None),
        P("section", "ctx", None),
        P("section", "ctx", None),
        P("section", "ctx", None),
        P("section", "ctx", None),
        P("section", "ctx", None),
        P("section", "ctx", None),
        P("section", None, None),
    )
    return jax.shard_map(
        per_device,
        mesh=mesh,
        in_specs=placed,
        out_specs=(P("section", "ctx", None), P("section", "ctx", None), P("section", None, "ctx")),
        check_vma=False,
    )
```

```python
import functools
import math

import jax
import jax.numpy as jnp
from jax import lax
from jax.experimental import pallas as pl
from jax.experimental.pallas import tpu as pltpu
from jax.sharding import PartitionSpec as P

MESH_IDS = pl.DeviceIdType.MESH


def tap_exchange_kernel(nz, nx, nc, scale, x_ref, o_ref, r1, s1, r2, s2, r3, sems):
    me = lax.axis_index("ctx")
    sec = lax.axis_index("section")
    core = me % nc
    xi = (me // nc) % nx
    zi = me // (nc * nx)

    def device(z, x, c):
        return (sec, (z * nx + x) * nc + c)

    peers = [device(zi, xi, 1 - core)]
    peers += [device(zi, (xi + k) % nx, core) for k in range(1, nx)]
    peers += [device((zi + k) % nz, xi, core) for k in range(1, nz)]
    barrier = pltpu.get_barrier_semaphore()
    for peer in peers:
        pl.semaphore_signal(barrier, inc=1, device_id=peer, device_id_type=MESH_IDS)
    pl.semaphore_wait(barrier, len(peers))

    def send(src, dst, peer, out_slot, in_slot):
        return pltpu.make_async_remote_copy(
            src_ref=src,
            dst_ref=dst,
            send_sem=sems.at[0, out_slot],
            recv_sem=sems.at[1, in_slot],
            device_id=peer,
            device_id_type=MESH_IDS,
        )

    first = send(x_ref.at[:, :, 1 - core], r1, peers[0], 0, 0)
    first.start()
    first.wait()
    s1[...] = x_ref[:, :, core] + r1[...]

    second = []
    for k in range(1, nx):
        target = (xi + k) % nx
        copy = send(s1.at[:, target], r2.at[xi], device(zi, target, core), 1 + target, 1 + xi)
        copy.start()
        second.append(copy)
    for k in range(1, nx):
        source = (xi + nx - k) % nx
        send(s1.at[:, source], r2.at[source], device(zi, source, core), 1 + source, 1 + source).wait_recv()
    for copy in second:
        copy.wait_send()
    r2[xi] = s1[:, xi]
    s2[...] = jnp.sum(r2[...], axis=0)

    third = []
    for k in range(1, nz):
        target = (zi + k) % nz
        copy = send(s2.at[target], r3.at[zi], device(target, xi, core), 1 + nx + target, 1 + nx + zi)
        copy.start()
        third.append(copy)
    for k in range(1, nz):
        source = (zi + nz - k) % nz
        send(s2.at[source], r3.at[source], device(source, xi, core), 1 + nx + source, 1 + nx + source).wait_recv()
    for copy in third:
        copy.wait_send()
    r3[zi] = s2[zi]
    o_ref[...] = (jnp.sum(r3[...], axis=0) * scale).astype(o_ref.dtype)


def tap_exchange(parts, scale):
    nz, nx, nc, taps, width = parts.shape
    return pl.pallas_call(
        functools.partial(tap_exchange_kernel, nz, nx, nc, scale),
        out_shape=jax.ShapeDtypeStruct((taps, width), jnp.bfloat16),
        in_specs=[pl.BlockSpec(memory_space=pltpu.VMEM)],
        out_specs=pl.BlockSpec(memory_space=pltpu.VMEM),
        scratch_shapes=[
            pltpu.VMEM((nz, nx, taps, width), jnp.float32),
            pltpu.VMEM((nz, nx, taps, width), jnp.float32),
            pltpu.VMEM((nx, nz, taps, width), jnp.float32),
            pltpu.VMEM((nz, taps, width), jnp.float32),
            pltpu.VMEM((nz, taps, width), jnp.float32),
            pltpu.SemaphoreType.DMA((2, 1 + nx + nz)),
        ],
        compiler_params=pltpu.CompilerParams(collective_id=0, has_side_effects=True),
    )(parts)


def exchange_kernel(n, send_part, recv_part, x_ref, o_ref, local_sem, send_sems, recv_sems, *staged):
    if staged:
        (stage,) = staged
        for index in range(x_ref.shape[0]):
            stage[index] = x_ref[index].astype(jnp.float32).T.astype(stage.dtype)
        x_ref = stage
    me = lax.axis_index("ctx")
    sec = lax.axis_index("section")
    barrier = pltpu.get_barrier_semaphore()

    def greet(k, carry):
        peer = lax.rem(me + k, n)
        pl.semaphore_signal(barrier, inc=1, device_id=(sec, peer), device_id_type=MESH_IDS)
        return carry

    lax.fori_loop(1, n, greet, 0)
    pl.semaphore_wait(barrier, n - 1)

    def copy(peer, source):
        return pltpu.make_async_remote_copy(
            src_ref=send_part(x_ref, peer),
            dst_ref=recv_part(o_ref, source),
            send_sem=send_sems.at[peer],
            recv_sem=recv_sems.at[source],
            device_id=(sec, peer),
            device_id_type=MESH_IDS,
        )

    def start(k, carry):
        copy(lax.rem(me + k, n), me).start()
        return carry

    lax.fori_loop(1, n, start, 0)
    own = pltpu.make_async_copy(send_part(x_ref, me), recv_part(o_ref, me), local_sem)
    own.start()

    def finish(k, carry):
        copy(lax.rem(me + n - k, n), lax.rem(me + n - k, n)).wait_recv()
        copy(lax.rem(me + k, n), me).wait_send()
        return carry

    lax.fori_loop(1, n, finish, 0)
    own.wait()


def exchange(x, out_shape, send_part, recv_part, collective, staged=()):
    n = lax.axis_size("ctx")
    return pl.pallas_call(
        functools.partial(exchange_kernel, n, send_part, recv_part),
        out_shape=jax.ShapeDtypeStruct(out_shape, x.dtype),
        in_specs=[pl.BlockSpec(memory_space=pltpu.VMEM)],
        out_specs=pl.BlockSpec(memory_space=pltpu.VMEM),
        scratch_shapes=[
            pltpu.SemaphoreType.DMA(()),
            pltpu.SemaphoreType.DMA((n,)),
            pltpu.SemaphoreType.DMA((n,)),
            *staged,
        ],
        compiler_params=pltpu.CompilerParams(collective_id=collective, has_side_effects=True),
    )(x)


def to_channels(x):
    n = lax.axis_size("ctx")
    count, tokens, channels = x.shape
    rows = channels // n

    def send_part(ref, peer):
        return ref.at[:, pl.ds(pl.multiple_of(peer * rows, rows), rows), :]

    def recv_part(ref, source):
        return ref.at[:, :, pl.ds(pl.multiple_of(source * tokens, tokens), tokens)]

    stage = pltpu.VMEM((count, channels, tokens), x.dtype)
    return exchange(x, (count, rows, tokens * n), send_part, recv_part, 1, (stage,))


def to_positions(x):
    n = lax.axis_size("ctx")
    rows, length = x.shape
    tokens = length // n

    def send_part(ref, peer):
        return ref.at[:, pl.ds(pl.multiple_of(peer * tokens, tokens), tokens)]

    def recv_part(ref, source):
        return ref.at[pl.ds(pl.multiple_of(source * rows, rows), rows), :]

    return exchange(x, (rows * n, tokens), send_part, recv_part, 2)


def passed_along(value, axis, steps):
    count = lax.axis_size(axis)
    pairs = [(source, (source + steps) % count) for source in range(count)]
    return lax.ppermute(value, axis, pairs)


def shifted(array, axis, by):
    devices = lax.axis_size(axis)
    pairs = [(i, i + by) for i in range(devices) if 0 <= i + by < devices]
    return lax.ppermute(array, axis, pairs)


def unit_roots(rows, cols, period):
    row_ids = jnp.arange(rows, dtype=jnp.int32)[:, None]
    col_ids = jnp.arange(cols, dtype=jnp.int32)[None, :]
    angle = (row_ids * col_ids % period).astype(jnp.float32) * (-2.0 * math.pi / period)
    return (jnp.cos(angle), jnp.sin(angle))


def contract(form, left, right):
    return jnp.einsum(
        form, left, right, precision=lax.Precision.HIGH, preferred_element_type=jnp.float32
    )


def to_spectrum(parts, factor_a, factor_b):
    channels = parts.shape[0]
    inputs_count = parts.shape[1]
    half = factor_a // 2
    period = factor_a * factor_b
    fa_cos, fa_sin = unit_roots(factor_a, half, factor_a)
    first_table = jnp.stack([jnp.stack([fa_cos, -fa_sin]), jnp.stack([fa_sin, fa_cos])])[
        :, :inputs_count
    ]
    tw_cos, tw_sin = unit_roots(factor_a, factor_b, period)
    fb_cos, fb_sin = unit_roots(factor_b, factor_b, factor_b)
    second_table = jnp.stack([jnp.stack([fb_cos, fb_sin]), jnp.stack([-fb_sin, fb_cos])])
    shaped = parts.reshape(channels, inputs_count, half, factor_b)
    first = contract("qrca,nrab->nqcb", first_table, shaped)
    first_re = first[:, 0]
    first_im = first[:, 1]
    turned = jnp.stack(
        [first_re * tw_cos - first_im * tw_sin, first_re * tw_sin + first_im * tw_cos], 1
    )
    return contract("nqcb,qpbd->npcd", turned, second_table)


def from_spectrum(spectrum, factor_a, factor_b, scale):
    channels = spectrum.shape[0]
    half = factor_a // 2
    period = factor_a * factor_b
    fb_cos, fb_sin = unit_roots(factor_b, factor_b, factor_b)
    back_table = jnp.stack([jnp.stack([fb_cos, -fb_sin]), jnp.stack([fb_sin, fb_cos])])
    tw_cos, tw_sin = unit_roots(factor_a, factor_b, period)
    fa_cos, fa_sin = unit_roots(half, factor_a, factor_a)
    last_table = jnp.stack(
        [
            jnp.stack([fa_cos, fa_sin]) * (scale / period),
            jnp.stack([-fa_sin, fa_cos]) * (1.0 / period),
        ]
    )
    middle = contract("npcd,pqdb->nqcb", spectrum, back_table)
    middle_re = middle[:, 0]
    middle_im = middle[:, 1]
    turned = jnp.stack(
        [middle_re * tw_cos + middle_im * tw_sin, middle_im * tw_cos - middle_re * tw_sin], 1
    )
    result = contract("rqac,nqcb->nrab", last_table, turned)
    length = half * factor_b
    return (result[:, 0].reshape(channels, length), result[:, 1].reshape(channels, length))


def depthwise(extended, kernel):
    result = lax.conv_general_dilated(
        extended[None],
        kernel[:, None, :],
        (1,),
        "VALID",
        dimension_numbers=("NWC", "WIO", "NWC"),
        feature_group_count=extended.shape[1],
        preferred_element_type=jnp.float32,
    )
    return result[0]


def per_device(
    incoming, layer_input, pre_gate, mid_gate, long_gate, out_gate, long_filter, mid_filter
):
    sections = lax.axis_size("section")
    beta = (2.0 * sections) ** (-0.5)
    adjoint = passed_along(incoming[0], "section", -1).astype(jnp.float32)
    inputs = layer_input[0].astype(jnp.float32)
    tokens = inputs.shape[0]
    gate_pre = pre_gate[0].astype(jnp.float32)
    gate_mid = mid_gate[0].astype(jnp.float32)
    gate_long = long_gate[0].astype(jnp.float32)
    gate_out = out_gate[0].astype(jnp.float32)
    filter_taps = mid_filter[0]
    reach = filter_taps.shape[0] - 1
    seq_len = tokens * lax.axis_size("ctx")
    scale = float(seq_len) ** (-0.5)
    mixed_in = (inputs * gate_pre).astype(jnp.bfloat16)
    earlier = shifted(mixed_in[tokens - reach :], "ctx", 1)
    extended = jnp.concatenate([earlier, mixed_in], 0)
    flip = jnp.eye(filter_taps.shape[0], dtype=filter_taps.dtype)[::-1]
    flipped_taps = jnp.dot(flip, filter_taps, preferred_element_type=jnp.float32)
    branch = depthwise(extended, flipped_taps.astype(filter_taps.dtype))
    resid = inputs + beta * branch * gate_mid
    long_in = (resid * gate_long).astype(jnp.bfloat16)
    grad_z = (beta * adjoint * gate_out).astype(jnp.bfloat16)
    channel_z, channel_w = to_channels(jnp.stack([grad_z, long_in]))
    factor_b = math.gcd(seq_len, 128)
    factor_a = 2 * seq_len // factor_b
    zspec = to_spectrum(channel_z[:, None], factor_a, factor_b)
    zspec_re = zspec[:, 0]
    zspec_im = zspec[:, 1]
    pair = to_spectrum(jnp.stack([channel_w, -long_filter[0]], 1), factor_a, factor_b)
    pair_re = pair[:, 0]
    pair_im = pair[:, 1]
    joint_re = zspec_re * pair_re + zspec_im * pair_im
    joint_im = zspec_im * pair_re - zspec_re * pair_im
    lag_grad, input_part = from_spectrum(
        jnp.stack([joint_re, joint_im], 1), factor_a, factor_b, scale
    )
    long_grad = lag_grad.astype(jnp.bfloat16)[None]
    returned = lax.all_to_all(
        input_part.astype(jnp.bfloat16), "ctx", split_axis=1, concat_axis=0, tiled=True
    ).T
    grad_u = adjoint + returned.astype(jnp.float32) * gate_long
    grad_b = (beta * grad_u * gate_mid).astype(jnp.bfloat16)
    later = shifted(grad_b[:reach], "ctx", -1)
    grad_act = depthwise(jnp.concatenate([grad_b, later], 0), filter_taps)
    input_grad = (grad_u + grad_act * gate_pre).astype(jnp.bfloat16)[None]
    tap_part = lax.conv_general_dilated(
        extended[None],
        grad_b[:, None, :],
        (1,),
        "VALID",
        dimension_numbers=("NWC", "WIO", "NCW"),
        feature_group_count=extended.shape[1],
        preferred_element_type=jnp.float32,
    )[0]
    devices = lax.axis_size("ctx")
    columns = tap_part.shape[0] // devices
    chip_cores, chips_x = 2, 4
    chips_z = devices // (chip_cores * chips_x)
    parts = tap_part.reshape(chips_z, chips_x, chip_cores, columns, tap_part.shape[1])
    mid_grad = tap_exchange(parts, scale).T[::-1][None]
    return (input_grad, long_grad, mid_grad)


def solution(mesh):
    placed = (
        P("section", "ctx", None),
        P("section", "ctx", None),
        P("section", "ctx", None),
        P("section", "ctx", None),
        P("section", "ctx", None),
        P("section", "ctx", None),
        P("section", "ctx", None),
        P("section", None, None),
    )
    return jax.shard_map(
        per_device,
        mesh=mesh,
        in_specs=placed,
        out_specs=(P("section", "ctx", None), P("section", "ctx", None), P("section", None, "ctx")),
        check_vma=False,
    )
```

```python
import functools
import math

import jax
import jax.numpy as jnp
from jax import lax
from jax.experimental import pallas as pl
from jax.experimental.pallas import tpu as pltpu
from jax.sharding import PartitionSpec as P

MESH_IDS = pl.DeviceIdType.MESH


def tap_exchange_kernel(nz, nx, nc, scale, x_ref, o_ref, r1, s1, r2, s2, r3, sems):
    me = lax.axis_index("ctx")
    sec = lax.axis_index("section")
    core = me % nc
    xi = (me // nc) % nx
    zi = me // (nc * nx)

    def device(z, x, c):
        return (sec, (z * nx + x) * nc + c)

    peers = [device(zi, xi, 1 - core)]
    peers += [device(zi, (xi + k) % nx, core) for k in range(1, nx)]
    peers += [device((zi + k) % nz, xi, core) for k in range(1, nz)]
    barrier = pltpu.get_barrier_semaphore()
    for peer in peers:
        pl.semaphore_signal(barrier, inc=1, device_id=peer, device_id_type=MESH_IDS)
    pl.semaphore_wait(barrier, len(peers))

    def send(src, dst, peer, out_slot, in_slot):
        return pltpu.make_async_remote_copy(
            src_ref=src,
            dst_ref=dst,
            send_sem=sems.at[0, out_slot],
            recv_sem=sems.at[1, in_slot],
            device_id=peer,
            device_id_type=MESH_IDS,
        )

    first = send(x_ref.at[:, :, 1 - core], r1, peers[0], 0, 0)
    first.start()
    first.wait()
    s1[...] = x_ref[:, :, core] + r1[...]

    second = []
    for k in range(1, nx):
        target = (xi + k) % nx
        copy = send(s1.at[:, target], r2.at[xi], device(zi, target, core), 1 + target, 1 + xi)
        copy.start()
        second.append(copy)
    for k in range(1, nx):
        source = (xi + nx - k) % nx
        send(s1.at[:, source], r2.at[source], device(zi, source, core), 1 + source, 1 + source).wait_recv()
    for copy in second:
        copy.wait_send()
    r2[xi] = s1[:, xi]
    s2[...] = jnp.sum(r2[...], axis=0)

    third = []
    for k in range(1, nz):
        target = (zi + k) % nz
        copy = send(s2.at[target], r3.at[zi], device(target, xi, core), 1 + nx + target, 1 + nx + zi)
        copy.start()
        third.append(copy)
    for k in range(1, nz):
        source = (zi + nz - k) % nz
        send(s2.at[source], r3.at[source], device(source, xi, core), 1 + nx + source, 1 + nx + source).wait_recv()
    for copy in third:
        copy.wait_send()
    r3[zi] = s2[zi]
    o_ref[...] = (jnp.sum(r3[...], axis=0) * scale).astype(o_ref.dtype)


def tap_exchange(parts, scale):
    nz, nx, nc, taps, width = parts.shape
    return pl.pallas_call(
        functools.partial(tap_exchange_kernel, nz, nx, nc, scale),
        out_shape=jax.ShapeDtypeStruct((taps, width), jnp.bfloat16),
        in_specs=[pl.BlockSpec(memory_space=pltpu.VMEM)],
        out_specs=pl.BlockSpec(memory_space=pltpu.VMEM),
        scratch_shapes=[
            pltpu.VMEM((nz, nx, taps, width), jnp.float32),
            pltpu.VMEM((nz, nx, taps, width), jnp.float32),
            pltpu.VMEM((nx, nz, taps, width), jnp.float32),
            pltpu.VMEM((nz, taps, width), jnp.float32),
            pltpu.VMEM((nz, taps, width), jnp.float32),
            pltpu.SemaphoreType.DMA((2, 1 + nx + nz)),
        ],
        compiler_params=pltpu.CompilerParams(collective_id=0, has_side_effects=True),
    )(parts)


def channel_kernel(n, x_ref, o_ref, stage, local_sems, send_sems, recv_sems):
    count, channels, tokens = stage.shape
    rows = channels // n
    me = lax.axis_index("ctx")
    sec = lax.axis_index("section")
    barrier = pltpu.get_barrier_semaphore()

    def greet(k, carry):
        peer = lax.rem(me + k, n)
        pl.semaphore_signal(barrier, inc=1, device_id=(sec, peer), device_id_type=MESH_IDS)
        return carry

    lax.fori_loop(1, n, greet, 0)
    pl.semaphore_wait(barrier, n - 1)

    def copy(index, peer, source):
        return pltpu.make_async_remote_copy(
            src_ref=stage.at[index, pl.ds(pl.multiple_of(peer * rows, rows), rows), :],
            dst_ref=o_ref.at[index, :, pl.ds(pl.multiple_of(source * tokens, tokens), tokens)],
            send_sem=send_sems.at[index, peer],
            recv_sem=recv_sems.at[index, source],
            device_id=(sec, peer),
            device_id_type=MESH_IDS,
        )

    owns = []
    for index in range(count):
        stage[index] = x_ref[index].astype(jnp.float32).T.astype(stage.dtype)

        def start(k, carry, index=index):
            copy(index, lax.rem(me + k, n), me).start()
            return carry

        lax.fori_loop(1, n, start, 0)
        own = pltpu.make_async_copy(
            stage.at[index, pl.ds(pl.multiple_of(me * rows, rows), rows), :],
            o_ref.at[index, :, pl.ds(pl.multiple_of(me * tokens, tokens), tokens)],
            local_sems.at[index],
        )
        own.start()
        owns.append(own)

    for index in range(count):

        def finish(k, carry, index=index):
            source = lax.rem(me + n - k, n)
            copy(index, source, source).wait_recv()
            copy(index, lax.rem(me + k, n), me).wait_send()
            return carry

        lax.fori_loop(1, n, finish, 0)
        owns[index].wait()


def to_channels(x):
    n = lax.axis_size("ctx")
    count, tokens, channels = x.shape
    return pl.pallas_call(
        functools.partial(channel_kernel, n),
        out_shape=jax.ShapeDtypeStruct((count, channels // n, tokens * n), x.dtype),
        in_specs=[pl.BlockSpec(memory_space=pltpu.VMEM)],
        out_specs=pl.BlockSpec(memory_space=pltpu.VMEM),
        scratch_shapes=[
            pltpu.VMEM((count, channels, tokens), x.dtype),
            pltpu.SemaphoreType.DMA((count,)),
            pltpu.SemaphoreType.DMA((count, n)),
            pltpu.SemaphoreType.DMA((count, n)),
        ],
        compiler_params=pltpu.CompilerParams(collective_id=1, has_side_effects=True),
    )(x)


def passed_along(value, axis, steps):
    count = lax.axis_size(axis)
    pairs = [(source, (source + steps) % count) for source in range(count)]
    return lax.ppermute(value, axis, pairs)


def shifted(array, axis, by):
    devices = lax.axis_size(axis)
    pairs = [(i, i + by) for i in range(devices) if 0 <= i + by < devices]
    return lax.ppermute(array, axis, pairs)


def unit_roots(rows, cols, period):
    row_ids = jnp.arange(rows, dtype=jnp.int32)[:, None]
    col_ids = jnp.arange(cols, dtype=jnp.int32)[None, :]
    angle = (row_ids * col_ids % period).astype(jnp.float32) * (-2.0 * math.pi / period)
    return (jnp.cos(angle), jnp.sin(angle))


def contract(form, left, right):
    return jnp.einsum(
        form, left, right, precision=lax.Precision.HIGH, preferred_element_type=jnp.float32
    )


def to_spectrum(parts, factor_a, factor_b):
    channels = parts.shape[0]
    inputs_count = parts.shape[1]
    half = factor_a // 2
    period = factor_a * factor_b
    fa_cos, fa_sin = unit_roots(factor_a, half, factor_a)
    first_table = jnp.stack([jnp.stack([fa_cos, -fa_sin]), jnp.stack([fa_sin, fa_cos])])[
        :, :inputs_count
    ]
    tw_cos, tw_sin = unit_roots(factor_a, factor_b, period)
    fb_cos, fb_sin = unit_roots(factor_b, factor_b, factor_b)
    second_table = jnp.stack([jnp.stack([fb_cos, fb_sin]), jnp.stack([-fb_sin, fb_cos])])
    shaped = parts.reshape(channels, inputs_count, half, factor_b)
    first = contract("qrca,nrab->nqcb", first_table, shaped)
    first_re = first[:, 0]
    first_im = first[:, 1]
    turned = jnp.stack(
        [first_re * tw_cos - first_im * tw_sin, first_re * tw_sin + first_im * tw_cos], 1
    )
    return contract("nqcb,qpbd->npcd", turned, second_table)


def from_spectrum(spectrum, factor_a, factor_b, scale):
    channels = spectrum.shape[0]
    half = factor_a // 2
    period = factor_a * factor_b
    fb_cos, fb_sin = unit_roots(factor_b, factor_b, factor_b)
    back_table = jnp.stack([jnp.stack([fb_cos, -fb_sin]), jnp.stack([fb_sin, fb_cos])])
    tw_cos, tw_sin = unit_roots(factor_a, factor_b, period)
    fa_cos, fa_sin = unit_roots(half, factor_a, factor_a)
    last_table = jnp.stack(
        [
            jnp.stack([fa_cos, fa_sin]) * (scale / period),
            jnp.stack([-fa_sin, fa_cos]) * (1.0 / period),
        ]
    )
    middle = contract("npcd,pqdb->nqcb", spectrum, back_table)
    middle_re = middle[:, 0]
    middle_im = middle[:, 1]
    turned = jnp.stack(
        [middle_re * tw_cos + middle_im * tw_sin, middle_im * tw_cos - middle_re * tw_sin], 1
    )
    result = contract("rqac,nqcb->nrab", last_table, turned)
    length = half * factor_b
    return (result[:, 0].reshape(channels, length), result[:, 1].reshape(channels, length))


def depthwise(extended, kernel):
    result = lax.conv_general_dilated(
        extended[None],
        kernel[:, None, :],
        (1,),
        "VALID",
        dimension_numbers=("NWC", "WIO", "NWC"),
        feature_group_count=extended.shape[1],
        preferred_element_type=jnp.float32,
    )
    return result[0]


def per_device(
    incoming, layer_input, pre_gate, mid_gate, long_gate, out_gate, long_filter, mid_filter
):
    sections = lax.axis_size("section")
    beta = (2.0 * sections) ** (-0.5)
    adjoint = passed_along(incoming[0], "section", -1).astype(jnp.float32)
    inputs = layer_input[0].astype(jnp.float32)
    tokens = inputs.shape[0]
    gate_pre = pre_gate[0].astype(jnp.float32)
    gate_mid = mid_gate[0].astype(jnp.float32)
    gate_long = long_gate[0].astype(jnp.float32)
    gate_out = out_gate[0].astype(jnp.float32)
    filter_taps = mid_filter[0]
    reach = filter_taps.shape[0] - 1
    seq_len = tokens * lax.axis_size("ctx")
    scale = float(seq_len) ** (-0.5)
    mixed_in = (inputs * gate_pre).astype(jnp.bfloat16)
    earlier = shifted(mixed_in[tokens - reach :], "ctx", 1)
    extended = jnp.concatenate([earlier, mixed_in], 0)
    flip = jnp.eye(filter_taps.shape[0], dtype=filter_taps.dtype)[::-1]
    flipped_taps = jnp.dot(flip, filter_taps, preferred_element_type=jnp.float32)
    branch = depthwise(extended, flipped_taps.astype(filter_taps.dtype))
    resid = inputs + beta * branch * gate_mid
    long_in = (resid * gate_long).astype(jnp.bfloat16)
    grad_z = (beta * adjoint * gate_out).astype(jnp.bfloat16)
    channel_z, channel_w = to_channels(jnp.stack([grad_z, long_in]))
    factor_b = math.gcd(seq_len, 128)
    factor_a = 2 * seq_len // factor_b
    zspec = to_spectrum(channel_z[:, None], factor_a, factor_b)
    zspec_re = zspec[:, 0]
    zspec_im = zspec[:, 1]
    pair = to_spectrum(jnp.stack([channel_w, -long_filter[0]], 1), factor_a, factor_b)
    pair_re = pair[:, 0]
    pair_im = pair[:, 1]
    joint_re = zspec_re * pair_re + zspec_im * pair_im
    joint_im = zspec_im * pair_re - zspec_re * pair_im
    lag_grad, input_part = from_spectrum(
        jnp.stack([joint_re, joint_im], 1), factor_a, factor_b, scale
    )
    long_grad = lag_grad.astype(jnp.bfloat16)[None]
    returned = lax.all_to_all(
        input_part.astype(jnp.bfloat16), "ctx", split_axis=1, concat_axis=0, tiled=True
    ).T
    grad_u = adjoint + returned.astype(jnp.float32) * gate_long
    grad_b = (beta * grad_u * gate_mid).astype(jnp.bfloat16)
    later = shifted(grad_b[:reach], "ctx", -1)
    grad_act = depthwise(jnp.concatenate([grad_b, later], 0), filter_taps)
    input_grad = (grad_u + grad_act * gate_pre).astype(jnp.bfloat16)[None]
    tap_part = lax.conv_general_dilated(
        extended[None],
        grad_b[:, None, :],
        (1,),
        "VALID",
        dimension_numbers=("NWC", "WIO", "NCW"),
        feature_group_count=extended.shape[1],
        preferred_element_type=jnp.float32,
    )[0]
    devices = lax.axis_size("ctx")
    columns = tap_part.shape[0] // devices
    chip_cores, chips_x = 2, 4
    chips_z = devices // (chip_cores * chips_x)
    parts = tap_part.reshape(chips_z, chips_x, chip_cores, columns, tap_part.shape[1])
    mid_grad = tap_exchange(parts, scale).T[::-1][None]
    return (input_grad, long_grad, mid_grad)


def solution(mesh):
    placed = (
        P("section", "ctx", None),
        P("section", "ctx", None),
        P("section", "ctx", None),
        P("section", "ctx", None),
        P("section", "ctx", None),
        P("section", "ctx", None),
        P("section", "ctx", None),
        P("section", None, None),
    )
    return jax.shard_map(
        per_device,
        mesh=mesh,
        in_specs=placed,
        out_specs=(P("section", "ctx", None), P("section", "ctx", None), P("section", None, "ctx")),
        check_vma=False,
    )
```

```python
import functools
import math

import jax
import jax.numpy as jnp
from jax import lax
from jax.experimental import pallas as pl
from jax.experimental.pallas import tpu as pltpu
from jax.sharding import PartitionSpec as P

MESH_IDS = pl.DeviceIdType.MESH


def tap_exchange_kernel(nz, nx, nc, scale, x_ref, o_ref, r1, s1, r2, s2, r3, sems):
    me = lax.axis_index("ctx")
    sec = lax.axis_index("section")
    core = me % nc
    xi = (me // nc) % nx
    zi = me // (nc * nx)

    def device(z, x, c):
        return (sec, (z * nx + x) * nc + c)

    peers = [device(zi, xi, 1 - core)]
    peers += [device(zi, (xi + k) % nx, core) for k in range(1, nx)]
    peers += [device((zi + k) % nz, xi, core) for k in range(1, nz)]
    barrier = pltpu.get_barrier_semaphore()
    for peer in peers:
        pl.semaphore_signal(barrier, inc=1, device_id=peer, device_id_type=MESH_IDS)
    pl.semaphore_wait(barrier, len(peers))

    def send(src, dst, peer, out_slot, in_slot):
        return pltpu.make_async_remote_copy(
            src_ref=src,
            dst_ref=dst,
            send_sem=sems.at[0, out_slot],
            recv_sem=sems.at[1, in_slot],
            device_id=peer,
            device_id_type=MESH_IDS,
        )

    first = send(x_ref.at[:, :, 1 - core], r1, peers[0], 0, 0)
    first.start()
    first.wait()
    s1[...] = x_ref[:, :, core] + r1[...]

    second = []
    for k in range(1, nx):
        target = (xi + k) % nx
        copy = send(s1.at[:, target], r2.at[xi], device(zi, target, core), 1 + target, 1 + xi)
        copy.start()
        second.append(copy)
    for k in range(1, nx):
        source = (xi + nx - k) % nx
        send(s1.at[:, source], r2.at[source], device(zi, source, core), 1 + source, 1 + source).wait_recv()
    for copy in second:
        copy.wait_send()
    r2[xi] = s1[:, xi]
    s2[...] = jnp.sum(r2[...], axis=0)

    third = []
    for k in range(1, nz):
        target = (zi + k) % nz
        copy = send(s2.at[target], r3.at[zi], device(target, xi, core), 1 + nx + target, 1 + nx + zi)
        copy.start()
        third.append(copy)
    for k in range(1, nz):
        source = (zi + nz - k) % nz
        send(s2.at[source], r3.at[source], device(source, xi, core), 1 + nx + source, 1 + nx + source).wait_recv()
    for copy in third:
        copy.wait_send()
    r3[zi] = s2[zi]
    o_ref[...] = (jnp.sum(r3[...], axis=0) * scale).astype(o_ref.dtype)


def tap_exchange(parts, scale):
    nz, nx, nc, taps, width = parts.shape
    return pl.pallas_call(
        functools.partial(tap_exchange_kernel, nz, nx, nc, scale),
        out_shape=jax.ShapeDtypeStruct((taps, width), jnp.bfloat16),
        in_specs=[pl.BlockSpec(memory_space=pltpu.VMEM)],
        out_specs=pl.BlockSpec(memory_space=pltpu.VMEM),
        scratch_shapes=[
            pltpu.VMEM((nz, nx, taps, width), jnp.float32),
            pltpu.VMEM((nz, nx, taps, width), jnp.float32),
            pltpu.VMEM((nx, nz, taps, width), jnp.float32),
            pltpu.VMEM((nz, taps, width), jnp.float32),
            pltpu.VMEM((nz, taps, width), jnp.float32),
            pltpu.SemaphoreType.DMA((2, 1 + nx + nz)),
        ],
        compiler_params=pltpu.CompilerParams(collective_id=0, has_side_effects=True),
    )(parts)


def channel_kernel(n, x_ref, o_ref, stage, local_sems, send_sems, recv_sems):
    count, channels, tokens = stage.shape
    rows = channels // n
    me = lax.axis_index("ctx")
    sec = lax.axis_index("section")
    barrier = pltpu.get_barrier_semaphore()

    def greet(k, carry):
        peer = lax.rem(me + k, n)
        pl.semaphore_signal(barrier, inc=1, device_id=(sec, peer), device_id_type=MESH_IDS)
        return carry

    lax.fori_loop(1, n, greet, 0)
    pl.semaphore_wait(barrier, n - 1)

    def copy(index, peer, source):
        return pltpu.make_async_remote_copy(
            src_ref=stage.at[index, pl.ds(pl.multiple_of(peer * rows, rows), rows), :],
            dst_ref=o_ref.at[index, :, pl.ds(pl.multiple_of(source * tokens, tokens), tokens)],
            send_sem=send_sems.at[index, peer],
            recv_sem=recv_sems.at[index, source],
            device_id=(sec, peer),
            device_id_type=MESH_IDS,
        )

    owns = []
    for index in range(count):
        stage[index] = x_ref[index].astype(jnp.float32).T.astype(stage.dtype)

        def start(k, carry, index=index):
            copy(index, lax.rem(me + k, n), me).start()
            return carry

        lax.fori_loop(1, n, start, 0)
        own = pltpu.make_async_copy(
            stage.at[index, pl.ds(pl.multiple_of(me * rows, rows), rows), :],
            o_ref.at[index, :, pl.ds(pl.multiple_of(me * tokens, tokens), tokens)],
            local_sems.at[index],
        )
        own.start()
        owns.append(own)

    for index in range(count):

        def finish(k, carry, index=index):
            source = lax.rem(me + n - k, n)
            copy(index, source, source).wait_recv()
            copy(index, lax.rem(me + k, n), me).wait_send()
            return carry

        lax.fori_loop(1, n, finish, 0)
        owns[index].wait()


def to_channels(x):
    n = lax.axis_size("ctx")
    count, tokens, channels = x.shape
    return pl.pallas_call(
        functools.partial(channel_kernel, n),
        out_shape=jax.ShapeDtypeStruct((count, channels // n, tokens * n), x.dtype),
        in_specs=[pl.BlockSpec(memory_space=pltpu.VMEM)],
        out_specs=pl.BlockSpec(memory_space=pltpu.VMEM),
        scratch_shapes=[
            pltpu.VMEM((count, channels, tokens), x.dtype),
            pltpu.SemaphoreType.DMA((count,)),
            pltpu.SemaphoreType.DMA((count, n)),
            pltpu.SemaphoreType.DMA((count, n)),
        ],
        compiler_params=pltpu.CompilerParams(collective_id=1, has_side_effects=True),
    )(x)


def passed_along(value, axis, steps):
    count = lax.axis_size(axis)
    pairs = [(source, (source + steps) % count) for source in range(count)]
    return lax.ppermute(value, axis, pairs)


def shifted(array, axis, by):
    devices = lax.axis_size(axis)
    pairs = [(i, i + by) for i in range(devices) if 0 <= i + by < devices]
    return lax.ppermute(array, axis, pairs)


def unit_roots(rows, cols, period):
    row_ids = jnp.arange(rows, dtype=jnp.int32)[:, None]
    col_ids = jnp.arange(cols, dtype=jnp.int32)[None, :]
    angle = (row_ids * col_ids % period).astype(jnp.float32) * (-2.0 * math.pi / period)
    return (jnp.cos(angle), jnp.sin(angle))


def contract(form, left, right):
    return jnp.einsum(
        form, left, right, precision=lax.Precision.HIGH, preferred_element_type=jnp.float32
    )


def to_spectrum(parts, factor_a, factor_b):
    channels = parts.shape[0]
    inputs_count = parts.shape[1]
    half = factor_a // 2
    period = factor_a * factor_b
    fa_cos, fa_sin = unit_roots(factor_a, half, factor_a)
    first_table = jnp.stack([jnp.stack([fa_cos, -fa_sin]), jnp.stack([fa_sin, fa_cos])])[
        :, :inputs_count
    ]
    tw_cos, tw_sin = unit_roots(factor_a, factor_b, period)
    fb_cos, fb_sin = unit_roots(factor_b, factor_b, factor_b)
    second_table = jnp.stack([jnp.stack([fb_cos, fb_sin]), jnp.stack([-fb_sin, fb_cos])])
    shaped = parts.reshape(channels, inputs_count, half, factor_b)
    first = contract("qrca,nrab->nqcb", first_table, shaped)
    first_re = first[:, 0]
    first_im = first[:, 1]
    turned = jnp.stack(
        [first_re * tw_cos - first_im * tw_sin, first_re * tw_sin + first_im * tw_cos], 1
    )
    return contract("nqcb,qpbd->npcd", turned, second_table)


def from_spectrum(spectrum, factor_a, factor_b, scale):
    channels = spectrum.shape[0]
    half = factor_a // 2
    period = factor_a * factor_b
    fb_cos, fb_sin = unit_roots(factor_b, factor_b, factor_b)
    back_table = jnp.stack([jnp.stack([fb_cos, -fb_sin]), jnp.stack([fb_sin, fb_cos])])
    tw_cos, tw_sin = unit_roots(factor_a, factor_b, period)
    fa_cos, fa_sin = unit_roots(half, factor_a, factor_a)
    last_table = jnp.stack(
        [
            jnp.stack([fa_cos, fa_sin]) * (scale / period),
            jnp.stack([-fa_sin, fa_cos]) * (1.0 / period),
        ]
    )
    middle = contract("npcd,pqdb->nqcb", spectrum, back_table)
    middle_re = middle[:, 0]
    middle_im = middle[:, 1]
    turned = jnp.stack(
        [middle_re * tw_cos + middle_im * tw_sin, middle_im * tw_cos - middle_re * tw_sin], 1
    )
    result = contract("rqac,nqcb->nrab", last_table, turned)
    length = half * factor_b
    return (result[:, 0].reshape(channels, length), result[:, 1].reshape(channels, length))


def depthwise(extended, kernel):
    result = lax.conv_general_dilated(
        extended[None],
        kernel[:, None, :],
        (1,),
        "VALID",
        dimension_numbers=("NWC", "WIO", "NWC"),
        feature_group_count=extended.shape[1],
        preferred_element_type=jnp.float32,
    )
    return result[0]


def per_device(
    incoming, layer_input, pre_gate, mid_gate, long_gate, out_gate, long_filter, mid_filter
):
    sections = lax.axis_size("section")
    beta = (2.0 * sections) ** (-0.5)
    adjoint = passed_along(incoming[0], "section", -1).astype(jnp.float32)
    inputs = layer_input[0].astype(jnp.float32)
    tokens = inputs.shape[0]
    gate_pre = pre_gate[0].astype(jnp.float32)
    gate_mid = mid_gate[0].astype(jnp.float32)
    gate_long = long_gate[0].astype(jnp.float32)
    gate_out = out_gate[0].astype(jnp.float32)
    filter_taps = mid_filter[0]
    reach = filter_taps.shape[0] - 1
    seq_len = tokens * lax.axis_size("ctx")
    scale = float(seq_len) ** (-0.5)
    mixed_in = (inputs * gate_pre).astype(jnp.bfloat16)
    earlier = shifted(mixed_in[tokens - reach :], "ctx", 1)
    extended = jnp.concatenate([earlier, mixed_in], 0)
    flip = jnp.eye(filter_taps.shape[0], dtype=filter_taps.dtype)[::-1]
    flipped_taps = jnp.dot(flip, filter_taps, preferred_element_type=jnp.float32)
    branch = depthwise(extended, flipped_taps.astype(filter_taps.dtype))
    resid = inputs + beta * branch * gate_mid
    long_in = (resid * gate_long).astype(jnp.bfloat16)
    grad_z = (beta * adjoint * gate_out).astype(jnp.bfloat16)
    channel_z, channel_w = to_channels(jnp.stack([grad_z, long_in]))
    factor_b = math.gcd(seq_len, 128)
    factor_a = 2 * seq_len // factor_b
    zspec = to_spectrum(channel_z[:, None], factor_a, factor_b)
    zspec_re = zspec[:, 0]
    zspec_im = zspec[:, 1]
    pair = to_spectrum(jnp.stack([channel_w, -long_filter[0]], 1), factor_a, factor_b)
    pair_re = pair[:, 0]
    pair_im = pair[:, 1]
    joint_re = zspec_re * pair_re + zspec_im * pair_im
    joint_im = zspec_im * pair_re - zspec_re * pair_im
    lag_grad, input_part = from_spectrum(
        jnp.stack([joint_re, joint_im], 1), factor_a, factor_b, scale
    )
    long_grad = lag_grad.astype(jnp.bfloat16)[None]
    returned = lax.all_to_all(
        input_part.astype(jnp.bfloat16), "ctx", split_axis=1, concat_axis=0, tiled=True
    ).T
    grad_u = adjoint + returned.astype(jnp.float32) * gate_long
    grad_b = (beta * grad_u * gate_mid).astype(jnp.bfloat16)
    later = shifted(grad_b[:reach], "ctx", -1)
    grad_act = depthwise(jnp.concatenate([grad_b, later], 0), filter_taps)
    input_grad = (grad_u + grad_act * gate_pre).astype(jnp.bfloat16)[None]
    tap_part = lax.conv_general_dilated(
        extended[None],
        grad_b[:, None, :],
        (1,),
        "VALID",
        dimension_numbers=("NWC", "WIO", "NCW"),
        feature_group_count=extended.shape[1],
        preferred_element_type=jnp.float32,
    )[0]
    devices = lax.axis_size("ctx")
    columns = tap_part.shape[0] // devices
    chip_cores, chips_x = 2, 4
    chips_z = devices // (chip_cores * chips_x)
    parts = tap_part.reshape(chips_z, chips_x, chip_cores, columns, tap_part.shape[1])
    summed = tap_exchange(parts, scale)
    taps_flip = jnp.eye(summed.shape[1], dtype=summed.dtype)[::-1]
    mid_grad = jnp.dot(summed, taps_flip, preferred_element_type=jnp.float32)
    mid_grad = mid_grad.astype(summed.dtype).T[None]
    return (input_grad, long_grad, mid_grad)


def solution(mesh):
    placed = (
        P("section", "ctx", None),
        P("section", "ctx", None),
        P("section", "ctx", None),
        P("section", "ctx", None),
        P("section", "ctx", None),
        P("section", "ctx", None),
        P("section", "ctx", None),
        P("section", None, None),
    )
    return jax.shard_map(
        per_device,
        mesh=mesh,
        in_specs=placed,
        out_specs=(P("section", "ctx", None), P("section", "ctx", None), P("section", None, "ctx")),
        check_vma=False,
    )
```

```python
import functools
import math

import jax
import jax.numpy as jnp
from jax import lax
from jax.experimental import pallas as pl
from jax.experimental.pallas import tpu as pltpu
from jax.sharding import PartitionSpec as P

MESH_IDS = pl.DeviceIdType.MESH


def tap_exchange_kernel(nz, nx, nc, scale, x_ref, o_ref, r1, s1, r2, s2, r3, sems):
    me = lax.axis_index("ctx")
    sec = lax.axis_index("section")
    core = me % nc
    xi = (me // nc) % nx
    zi = me // (nc * nx)

    def device(z, x, c):
        return (sec, (z * nx + x) * nc + c)

    peers = [device(zi, xi, 1 - core)]
    peers += [device(zi, (xi + k) % nx, core) for k in range(1, nx)]
    peers += [device((zi + k) % nz, xi, core) for k in range(1, nz)]
    barrier = pltpu.get_barrier_semaphore()
    for peer in peers:
        pl.semaphore_signal(barrier, inc=1, device_id=peer, device_id_type=MESH_IDS)
    pl.semaphore_wait(barrier, len(peers))

    def send(src, dst, peer, out_slot, in_slot):
        return pltpu.make_async_remote_copy(
            src_ref=src,
            dst_ref=dst,
            send_sem=sems.at[0, out_slot],
            recv_sem=sems.at[1, in_slot],
            device_id=peer,
            device_id_type=MESH_IDS,
        )

    firsts = []
    for target in range(nx):
        copy = send(x_ref.at[:, target, 1 - core], r1.at[:, target], peers[0], target, target)
        copy.start()
        firsts.append(copy)
    second = []
    for k in range(1, nx + 1):
        target = (xi + k) % nx
        for block in range(nx):

            @pl.when(target == block)
            def _(block=block):
                firsts[block].wait()

        s1[:, target] = x_ref[:, target, core] + r1[:, target]
        if k < nx:
            copy = send(s1.at[:, target], r2.at[xi], device(zi, target, core), nx + target, nx + xi)
            copy.start()
            second.append(copy)
    for k in range(1, nx):
        source = (xi + nx - k) % nx
        send(s1.at[:, source], r2.at[source], device(zi, source, core), nx + source, nx + source).wait_recv()
    for copy in second:
        copy.wait_send()
    r2[xi] = s1[:, xi]
    s2[...] = jnp.sum(r2[...], axis=0)

    third = []
    for k in range(1, nz):
        target = (zi + k) % nz
        copy = send(s2.at[target], r3.at[zi], device(target, xi, core), 2 * nx + target, 2 * nx + zi)
        copy.start()
        third.append(copy)
    for k in range(1, nz):
        source = (zi + nz - k) % nz
        send(s2.at[source], r3.at[source], device(source, xi, core), 2 * nx + source, 2 * nx + source).wait_recv()
    for copy in third:
        copy.wait_send()
    r3[zi] = s2[zi]
    o_ref[...] = (jnp.sum(r3[...], axis=0) * scale).astype(o_ref.dtype)


def tap_exchange(parts, scale):
    nz, nx, nc, taps, width = parts.shape
    return pl.pallas_call(
        functools.partial(tap_exchange_kernel, nz, nx, nc, scale),
        out_shape=jax.ShapeDtypeStruct((taps, width), jnp.bfloat16),
        in_specs=[pl.BlockSpec(memory_space=pltpu.VMEM)],
        out_specs=pl.BlockSpec(memory_space=pltpu.VMEM),
        scratch_shapes=[
            pltpu.VMEM((nz, nx, taps, width), jnp.float32),
            pltpu.VMEM((nz, nx, taps, width), jnp.float32),
            pltpu.VMEM((nx, nz, taps, width), jnp.float32),
            pltpu.VMEM((nz, taps, width), jnp.float32),
            pltpu.VMEM((nz, taps, width), jnp.float32),
            pltpu.SemaphoreType.DMA((2, 2 * nx + nz)),
        ],
        compiler_params=pltpu.CompilerParams(collective_id=0, has_side_effects=True),
    )(parts)


def channel_kernel(n, x_ref, o_ref, stage, local_sems, send_sems, recv_sems):
    count, channels, tokens = stage.shape
    rows = channels // n
    me = lax.axis_index("ctx")
    sec = lax.axis_index("section")
    barrier = pltpu.get_barrier_semaphore()

    def greet(k, carry):
        peer = lax.rem(me + k, n)
        pl.semaphore_signal(barrier, inc=1, device_id=(sec, peer), device_id_type=MESH_IDS)
        return carry

    lax.fori_loop(1, n, greet, 0)
    pl.semaphore_wait(barrier, n - 1)

    def copy(index, peer, source):
        return pltpu.make_async_remote_copy(
            src_ref=stage.at[index, pl.ds(pl.multiple_of(peer * rows, rows), rows), :],
            dst_ref=o_ref.at[index, :, pl.ds(pl.multiple_of(source * tokens, tokens), tokens)],
            send_sem=send_sems.at[index, peer],
            recv_sem=recv_sems.at[index, source],
            device_id=(sec, peer),
            device_id_type=MESH_IDS,
        )

    owns = []
    for index in range(count):
        stage[index] = x_ref[index].astype(jnp.float32).T.astype(stage.dtype)

        def start(k, carry, index=index):
            copy(index, lax.rem(me + k, n), me).start()
            return carry

        lax.fori_loop(1, n, start, 0)
        own = pltpu.make_async_copy(
            stage.at[index, pl.ds(pl.multiple_of(me * rows, rows), rows), :],
            o_ref.at[index, :, pl.ds(pl.multiple_of(me * tokens, tokens), tokens)],
            local_sems.at[index],
        )
        own.start()
        owns.append(own)

    for index in range(count):

        def finish(k, carry, index=index):
            source = lax.rem(me + n - k, n)
            copy(index, source, source).wait_recv()
            copy(index, lax.rem(me + k, n), me).wait_send()
            return carry

        lax.fori_loop(1, n, finish, 0)
        owns[index].wait()


def to_channels(x):
    n = lax.axis_size("ctx")
    count, tokens, channels = x.shape
    return pl.pallas_call(
        functools.partial(channel_kernel, n),
        out_shape=jax.ShapeDtypeStruct((count, channels // n, tokens * n), x.dtype),
        in_specs=[pl.BlockSpec(memory_space=pltpu.VMEM)],
        out_specs=pl.BlockSpec(memory_space=pltpu.VMEM),
        scratch_shapes=[
            pltpu.VMEM((count, channels, tokens), x.dtype),
            pltpu.SemaphoreType.DMA((count,)),
            pltpu.SemaphoreType.DMA((count, n)),
            pltpu.SemaphoreType.DMA((count, n)),
        ],
        compiler_params=pltpu.CompilerParams(collective_id=1, has_side_effects=True),
    )(x)


def passed_along(value, axis, steps):
    count = lax.axis_size(axis)
    pairs = [(source, (source + steps) % count) for source in range(count)]
    return lax.ppermute(value, axis, pairs)


def shifted(array, axis, by):
    devices = lax.axis_size(axis)
    pairs = [(i, i + by) for i in range(devices) if 0 <= i + by < devices]
    return lax.ppermute(array, axis, pairs)


def unit_roots(rows, cols, period):
    row_ids = jnp.arange(rows, dtype=jnp.int32)[:, None]
    col_ids = jnp.arange(cols, dtype=jnp.int32)[None, :]
    angle = (row_ids * col_ids % period).astype(jnp.float32) * (-2.0 * math.pi / period)
    return (jnp.cos(angle), jnp.sin(angle))


def contract(form, left, right):
    return jnp.einsum(
        form, left, right, precision=lax.Precision.HIGH, preferred_element_type=jnp.float32
    )


def to_spectrum(parts, factor_a, factor_b):
    channels = parts.shape[0]
    inputs_count = parts.shape[1]
    half = factor_a // 2
    period = factor_a * factor_b
    fa_cos, fa_sin = unit_roots(factor_a, half, factor_a)
    first_table = jnp.stack([jnp.stack([fa_cos, -fa_sin]), jnp.stack([fa_sin, fa_cos])])[
        :, :inputs_count
    ]
    tw_cos, tw_sin = unit_roots(factor_a, factor_b, period)
    fb_cos, fb_sin = unit_roots(factor_b, factor_b, factor_b)
    second_table = jnp.stack([jnp.stack([fb_cos, fb_sin]), jnp.stack([-fb_sin, fb_cos])])
    shaped = parts.reshape(channels, inputs_count, half, factor_b)
    first = contract("qrca,nrab->nqcb", first_table, shaped)
    first_re = first[:, 0]
    first_im = first[:, 1]
    turned = jnp.stack(
        [first_re * tw_cos - first_im * tw_sin, first_re * tw_sin + first_im * tw_cos], 1
    )
    return contract("nqcb,qpbd->npcd", turned, second_table)


def from_spectrum(spectrum, factor_a, factor_b, scale):
    channels = spectrum.shape[0]
    half = factor_a // 2
    period = factor_a * factor_b
    fb_cos, fb_sin = unit_roots(factor_b, factor_b, factor_b)
    back_table = jnp.stack([jnp.stack([fb_cos, -fb_sin]), jnp.stack([fb_sin, fb_cos])])
    tw_cos, tw_sin = unit_roots(factor_a, factor_b, period)
    fa_cos, fa_sin = unit_roots(half, factor_a, factor_a)
    last_table = jnp.stack(
        [
            jnp.stack([fa_cos, fa_sin]) * (scale / period),
            jnp.stack([-fa_sin, fa_cos]) * (1.0 / period),
        ]
    )
    middle = contract("npcd,pqdb->nqcb", spectrum, back_table)
    middle_re = middle[:, 0]
    middle_im = middle[:, 1]
    turned = jnp.stack(
        [middle_re * tw_cos + middle_im * tw_sin, middle_im * tw_cos - middle_re * tw_sin], 1
    )
    result = contract("rqac,nqcb->nrab", last_table, turned)
    length = half * factor_b
    return (result[:, 0].reshape(channels, length), result[:, 1].reshape(channels, length))


def depthwise(extended, kernel):
    result = lax.conv_general_dilated(
        extended[None],
        kernel[:, None, :],
        (1,),
        "VALID",
        dimension_numbers=("NWC", "WIO", "NWC"),
        feature_group_count=extended.shape[1],
        preferred_element_type=jnp.float32,
    )
    return result[0]


def per_device(
    incoming, layer_input, pre_gate, mid_gate, long_gate, out_gate, long_filter, mid_filter
):
    sections = lax.axis_size("section")
    beta = (2.0 * sections) ** (-0.5)
    adjoint = passed_along(incoming[0], "section", -1).astype(jnp.float32)
    inputs = layer_input[0].astype(jnp.float32)
    tokens = inputs.shape[0]
    gate_pre = pre_gate[0].astype(jnp.float32)
    gate_mid = mid_gate[0].astype(jnp.float32)
    gate_long = long_gate[0].astype(jnp.float32)
    gate_out = out_gate[0].astype(jnp.float32)
    filter_taps = mid_filter[0]
    reach = filter_taps.shape[0] - 1
    seq_len = tokens * lax.axis_size("ctx")
    scale = float(seq_len) ** (-0.5)
    mixed_in = (inputs * gate_pre).astype(jnp.bfloat16)
    earlier = shifted(mixed_in[tokens - reach :], "ctx", 1)
    extended = jnp.concatenate([earlier, mixed_in], 0)
    flip = jnp.eye(filter_taps.shape[0], dtype=filter_taps.dtype)[::-1]
    flipped_taps = jnp.dot(flip, filter_taps, preferred_element_type=jnp.float32)
    branch = depthwise(extended, flipped_taps.astype(filter_taps.dtype))
    resid = inputs + beta * branch * gate_mid
    long_in = (resid * gate_long).astype(jnp.bfloat16)
    grad_z = (beta * adjoint * gate_out).astype(jnp.bfloat16)
    channel_z, channel_w = to_channels(jnp.stack([grad_z, long_in]))
    factor_b = math.gcd(seq_len, 128)
    factor_a = 2 * seq_len // factor_b
    zspec = to_spectrum(channel_z[:, None], factor_a, factor_b)
    zspec_re = zspec[:, 0]
    zspec_im = zspec[:, 1]
    pair = to_spectrum(jnp.stack([channel_w, -long_filter[0]], 1), factor_a, factor_b)
    pair_re = pair[:, 0]
    pair_im = pair[:, 1]
    joint_re = zspec_re * pair_re + zspec_im * pair_im
    joint_im = zspec_im * pair_re - zspec_re * pair_im
    lag_grad, input_part = from_spectrum(
        jnp.stack([joint_re, joint_im], 1), factor_a, factor_b, scale
    )
    long_grad = lag_grad.astype(jnp.bfloat16)[None]
    returned = lax.all_to_all(
        input_part.astype(jnp.bfloat16), "ctx", split_axis=1, concat_axis=0, tiled=True
    ).T
    grad_u = adjoint + returned.astype(jnp.float32) * gate_long
    grad_b = (beta * grad_u * gate_mid).astype(jnp.bfloat16)
    later = shifted(grad_b[:reach], "ctx", -1)
    grad_act = depthwise(jnp.concatenate([grad_b, later], 0), filter_taps)
    input_grad = (grad_u + grad_act * gate_pre).astype(jnp.bfloat16)[None]
    tap_part = lax.conv_general_dilated(
        extended[None],
        grad_b[:, None, :],
        (1,),
        "VALID",
        dimension_numbers=("NWC", "WIO", "NCW"),
        feature_group_count=extended.shape[1],
        preferred_element_type=jnp.float32,
    )[0]
    devices = lax.axis_size("ctx")
    columns = tap_part.shape[0] // devices
    chip_cores, chips_x = 2, 4
    chips_z = devices // (chip_cores * chips_x)
    parts = tap_part.reshape(chips_z, chips_x, chip_cores, columns, tap_part.shape[1])
    summed = tap_exchange(parts, scale)
    taps_flip = jnp.eye(summed.shape[1], dtype=summed.dtype)[::-1]
    mid_grad = jnp.dot(summed, taps_flip, preferred_element_type=jnp.float32)
    mid_grad = mid_grad.astype(summed.dtype).T[None]
    return (input_grad, long_grad, mid_grad)


def solution(mesh):
    placed = (
        P("section", "ctx", None),
        P("section", "ctx", None),
        P("section", "ctx", None),
        P("section", "ctx", None),
        P("section", "ctx", None),
        P("section", "ctx", None),
        P("section", "ctx", None),
        P("section", None, None),
    )
    return jax.shard_map(
        per_device,
        mesh=mesh,
        in_specs=placed,
        out_specs=(P("section", "ctx", None), P("section", "ctx", None), P("section", None, "ctx")),
        check_vma=False,
    )
```

```python
import functools
import math

import jax
import jax.numpy as jnp
from jax import lax
from jax.experimental import pallas as pl
from jax.experimental.pallas import tpu as pltpu
from jax.sharding import PartitionSpec as P

MESH_IDS = pl.DeviceIdType.MESH


def tap_exchange_kernel(nz, nx, nc, scale, x_ref, o_ref, r1, s1, r2, s2, r3, sems):
    me = lax.axis_index("ctx")
    sec = lax.axis_index("section")
    core = me % nc
    xi = (me // nc) % nx
    zi = me // (nc * nx)

    def device(z, x, c):
        return (sec, (z * nx + x) * nc + c)

    peers = [device(zi, xi, 1 - core)]
    peers += [device(zi, (xi + k) % nx, core) for k in range(1, nx)]
    peers += [device((zi + k) % nz, xi, core) for k in range(1, nz)]
    barrier = pltpu.get_barrier_semaphore()
    for peer in peers:
        pl.semaphore_signal(barrier, inc=1, device_id=peer, device_id_type=MESH_IDS)
    pl.semaphore_wait(barrier, len(peers))

    def send(src, dst, peer, out_slot, in_slot):
        return pltpu.make_async_remote_copy(
            src_ref=src,
            dst_ref=dst,
            send_sem=sems.at[0, out_slot],
            recv_sem=sems.at[1, in_slot],
            device_id=peer,
            device_id_type=MESH_IDS,
        )

    first = send(x_ref.at[:, :, 1 - core], r1, peers[0], 0, 0)
    first.start()
    first.wait()
    s1[...] = x_ref[:, :, core] + r1[...]

    second = []
    for k in range(1, nx):
        target = (xi + k) % nx
        copy = send(s1.at[:, target], r2.at[xi], device(zi, target, core), 1 + target, 1 + xi)
        copy.start()
        second.append(copy)
    for k in range(1, nx):
        source = (xi + nx - k) % nx
        send(s1.at[:, source], r2.at[source], device(zi, source, core), 1 + source, 1 + source).wait_recv()
    for copy in second:
        copy.wait_send()
    r2[xi] = s1[:, xi]
    s2[...] = jnp.sum(r2[...], axis=0)

    third = []
    for k in range(1, nz):
        target = (zi + k) % nz
        copy = send(s2.at[target], r3.at[zi], device(target, xi, core), 1 + nx + target, 1 + nx + zi)
        copy.start()
        third.append(copy)
    for k in range(1, nz):
        source = (zi + nz - k) % nz
        send(s2.at[source], r3.at[source], device(source, xi, core), 1 + nx + source, 1 + nx + source).wait_recv()
    for copy in third:
        copy.wait_send()
    r3[zi] = s2[zi]
    o_ref[...] = (jnp.sum(r3[...], axis=0) * scale).astype(o_ref.dtype)


def tap_exchange(parts, scale):
    nz, nx, nc, taps, width = parts.shape
    return pl.pallas_call(
        functools.partial(tap_exchange_kernel, nz, nx, nc, scale),
        out_shape=jax.ShapeDtypeStruct((taps, width), jnp.bfloat16),
        in_specs=[pl.BlockSpec(memory_space=pltpu.VMEM)],
        out_specs=pl.BlockSpec(memory_space=pltpu.VMEM),
        scratch_shapes=[
            pltpu.VMEM((nz, nx, taps, width), jnp.float32),
            pltpu.VMEM((nz, nx, taps, width), jnp.float32),
            pltpu.VMEM((nx, nz, taps, width), jnp.float32),
            pltpu.VMEM((nz, taps, width), jnp.float32),
            pltpu.VMEM((nz, taps, width), jnp.float32),
            pltpu.SemaphoreType.DMA((2, 1 + nx + nz)),
        ],
        compiler_params=pltpu.CompilerParams(collective_id=0, has_side_effects=True),
    )(parts)


def channel_kernel(n, x_ref, o_ref, stage, local_sems, send_sems, recv_sems):
    count, channels, tokens = stage.shape
    rows = channels // n
    me = lax.axis_index("ctx")
    sec = lax.axis_index("section")
    barrier = pltpu.get_barrier_semaphore()

    def greet(k, carry):
        peer = lax.rem(me + k, n)
        pl.semaphore_signal(barrier, inc=1, device_id=(sec, peer), device_id_type=MESH_IDS)
        return carry

    lax.fori_loop(1, n, greet, 0)
    pl.semaphore_wait(barrier, n - 1)

    def copy(index, peer, source):
        return pltpu.make_async_remote_copy(
            src_ref=stage.at[index, pl.ds(pl.multiple_of(peer * rows, rows), rows), :],
            dst_ref=o_ref.at[index, :, pl.ds(pl.multiple_of(source * tokens, tokens), tokens)],
            send_sem=send_sems.at[index, peer],
            recv_sem=recv_sems.at[index, source],
            device_id=(sec, peer),
            device_id_type=MESH_IDS,
        )

    owns = []
    for index in range(count):
        stage[index] = x_ref[index].astype(jnp.float32).T.astype(stage.dtype)

        def start(j, carry, index=index):
            odd = j % 2
            k = odd * ((j + 1) // 2) + (1 - odd) * (n - j // 2)
            copy(index, lax.rem(me + k, n), me).start()
            return carry

        lax.fori_loop(1, n, start, 0)
        own = pltpu.make_async_copy(
            stage.at[index, pl.ds(pl.multiple_of(me * rows, rows), rows), :],
            o_ref.at[index, :, pl.ds(pl.multiple_of(me * tokens, tokens), tokens)],
            local_sems.at[index],
        )
        own.start()
        owns.append(own)

    for index in range(count):

        def finish(k, carry, index=index):
            source = lax.rem(me + n - k, n)
            copy(index, source, source).wait_recv()
            copy(index, lax.rem(me + k, n), me).wait_send()
            return carry

        lax.fori_loop(1, n, finish, 0)
        owns[index].wait()


def to_channels(x):
    n = lax.axis_size("ctx")
    count, tokens, channels = x.shape
    return pl.pallas_call(
        functools.partial(channel_kernel, n),
        out_shape=jax.ShapeDtypeStruct((count, channels // n, tokens * n), x.dtype),
        in_specs=[pl.BlockSpec(memory_space=pltpu.VMEM)],
        out_specs=pl.BlockSpec(memory_space=pltpu.VMEM),
        scratch_shapes=[
            pltpu.VMEM((count, channels, tokens), x.dtype),
            pltpu.SemaphoreType.DMA((count,)),
            pltpu.SemaphoreType.DMA((count, n)),
            pltpu.SemaphoreType.DMA((count, n)),
        ],
        compiler_params=pltpu.CompilerParams(collective_id=1, has_side_effects=True),
    )(x)


def passed_along(value, axis, steps):
    count = lax.axis_size(axis)
    pairs = [(source, (source + steps) % count) for source in range(count)]
    return lax.ppermute(value, axis, pairs)


def shifted(array, axis, by):
    devices = lax.axis_size(axis)
    pairs = [(i, i + by) for i in range(devices) if 0 <= i + by < devices]
    return lax.ppermute(array, axis, pairs)


def unit_roots(rows, cols, period):
    row_ids = jnp.arange(rows, dtype=jnp.int32)[:, None]
    col_ids = jnp.arange(cols, dtype=jnp.int32)[None, :]
    angle = (row_ids * col_ids % period).astype(jnp.float32) * (-2.0 * math.pi / period)
    return (jnp.cos(angle), jnp.sin(angle))


def contract(form, left, right):
    return jnp.einsum(
        form, left, right, precision=lax.Precision.HIGH, preferred_element_type=jnp.float32
    )


def to_spectrum(parts, factor_a, factor_b):
    channels = parts.shape[0]
    inputs_count = parts.shape[1]
    half = factor_a // 2
    period = factor_a * factor_b
    fa_cos, fa_sin = unit_roots(factor_a, half, factor_a)
    first_table = jnp.stack([jnp.stack([fa_cos, -fa_sin]), jnp.stack([fa_sin, fa_cos])])[
        :, :inputs_count
    ]
    tw_cos, tw_sin = unit_roots(factor_a, factor_b, period)
    fb_cos, fb_sin = unit_roots(factor_b, factor_b, factor_b)
    second_table = jnp.stack([jnp.stack([fb_cos, fb_sin]), jnp.stack([-fb_sin, fb_cos])])
    shaped = parts.reshape(channels, inputs_count, half, factor_b)
    first = contract("qrca,nrab->nqcb", first_table, shaped)
    first_re = first[:, 0]
    first_im = first[:, 1]
    turned = jnp.stack(
        [first_re * tw_cos - first_im * tw_sin, first_re * tw_sin + first_im * tw_cos], 1
    )
    return contract("nqcb,qpbd->npcd", turned, second_table)


def from_spectrum(spectrum, factor_a, factor_b, scale):
    channels = spectrum.shape[0]
    half = factor_a // 2
    period = factor_a * factor_b
    fb_cos, fb_sin = unit_roots(factor_b, factor_b, factor_b)
    back_table = jnp.stack([jnp.stack([fb_cos, -fb_sin]), jnp.stack([fb_sin, fb_cos])])
    tw_cos, tw_sin = unit_roots(factor_a, factor_b, period)
    fa_cos, fa_sin = unit_roots(half, factor_a, factor_a)
    last_table = jnp.stack(
        [
            jnp.stack([fa_cos, fa_sin]) * (scale / period),
            jnp.stack([-fa_sin, fa_cos]) * (1.0 / period),
        ]
    )
    middle = contract("npcd,pqdb->nqcb", spectrum, back_table)
    middle_re = middle[:, 0]
    middle_im = middle[:, 1]
    turned = jnp.stack(
        [middle_re * tw_cos + middle_im * tw_sin, middle_im * tw_cos - middle_re * tw_sin], 1
    )
    result = contract("rqac,nqcb->nrab", last_table, turned)
    length = half * factor_b
    return (result[:, 0].reshape(channels, length), result[:, 1].reshape(channels, length))


def depthwise(extended, kernel):
    result = lax.conv_general_dilated(
        extended[None],
        kernel[:, None, :],
        (1,),
        "VALID",
        dimension_numbers=("NWC", "WIO", "NWC"),
        feature_group_count=extended.shape[1],
        preferred_element_type=jnp.float32,
    )
    return result[0]


def per_device(
    incoming, layer_input, pre_gate, mid_gate, long_gate, out_gate, long_filter, mid_filter
):
    sections = lax.axis_size("section")
    beta = (2.0 * sections) ** (-0.5)
    adjoint = passed_along(incoming[0], "section", -1).astype(jnp.float32)
    inputs = layer_input[0].astype(jnp.float32)
    tokens = inputs.shape[0]
    gate_pre = pre_gate[0].astype(jnp.float32)
    gate_mid = mid_gate[0].astype(jnp.float32)
    gate_long = long_gate[0].astype(jnp.float32)
    gate_out = out_gate[0].astype(jnp.float32)
    filter_taps = mid_filter[0]
    reach = filter_taps.shape[0] - 1
    seq_len = tokens * lax.axis_size("ctx")
    scale = float(seq_len) ** (-0.5)
    mixed_in = (inputs * gate_pre).astype(jnp.bfloat16)
    earlier = shifted(mixed_in[tokens - reach :], "ctx", 1)
    extended = jnp.concatenate([earlier, mixed_in], 0)
    flip = jnp.eye(filter_taps.shape[0], dtype=filter_taps.dtype)[::-1]
    flipped_taps = jnp.dot(flip, filter_taps, preferred_element_type=jnp.float32)
    branch = depthwise(extended, flipped_taps.astype(filter_taps.dtype))
    resid = inputs + beta * branch * gate_mid
    long_in = (resid * gate_long).astype(jnp.bfloat16)
    grad_z = (beta * adjoint * gate_out).astype(jnp.bfloat16)
    channel_z, channel_w = to_channels(jnp.stack([grad_z, long_in]))
    factor_b = math.gcd(seq_len, 128)
    factor_a = 2 * seq_len // factor_b
    zspec = to_spectrum(channel_z[:, None], factor_a, factor_b)
    zspec_re = zspec[:, 0]
    zspec_im = zspec[:, 1]
    pair = to_spectrum(jnp.stack([channel_w, -long_filter[0]], 1), factor_a, factor_b)
    pair_re = pair[:, 0]
    pair_im = pair[:, 1]
    joint_re = zspec_re * pair_re + zspec_im * pair_im
    joint_im = zspec_im * pair_re - zspec_re * pair_im
    lag_grad, input_part = from_spectrum(
        jnp.stack([joint_re, joint_im], 1), factor_a, factor_b, scale
    )
    long_grad = lag_grad.astype(jnp.bfloat16)[None]
    returned = lax.all_to_all(
        input_part.astype(jnp.bfloat16), "ctx", split_axis=1, concat_axis=0, tiled=True
    ).T
    grad_u = adjoint + returned.astype(jnp.float32) * gate_long
    grad_b = (beta * grad_u * gate_mid).astype(jnp.bfloat16)
    later = shifted(grad_b[:reach], "ctx", -1)
    grad_act = depthwise(jnp.concatenate([grad_b, later], 0), filter_taps)
    input_grad = (grad_u + grad_act * gate_pre).astype(jnp.bfloat16)[None]
    tap_part = lax.conv_general_dilated(
        extended[None],
        grad_b[:, None, :],
        (1,),
        "VALID",
        dimension_numbers=("NWC", "WIO", "NCW"),
        feature_group_count=extended.shape[1],
        preferred_element_type=jnp.float32,
    )[0]
    devices = lax.axis_size("ctx")
    columns = tap_part.shape[0] // devices
    chip_cores, chips_x = 2, 4
    chips_z = devices // (chip_cores * chips_x)
    parts = tap_part.reshape(chips_z, chips_x, chip_cores, columns, tap_part.shape[1])
    summed = tap_exchange(parts, scale)
    taps_flip = jnp.eye(summed.shape[1], dtype=summed.dtype)[::-1]
    mid_grad = jnp.dot(summed, taps_flip, preferred_element_type=jnp.float32)
    mid_grad = mid_grad.astype(summed.dtype).T[None]
    return (input_grad, long_grad, mid_grad)


def solution(mesh):
    placed = (
        P("section", "ctx", None),
        P("section", "ctx", None),
        P("section", "ctx", None),
        P("section", "ctx", None),
        P("section", "ctx", None),
        P("section", "ctx", None),
        P("section", "ctx", None),
        P("section", None, None),
    )
    return jax.shard_map(
        per_device,
        mesh=mesh,
        in_specs=placed,
        out_specs=(P("section", "ctx", None), P("section", "ctx", None), P("section", None, "ctx")),
        check_vma=False,
    )
```

```python
import functools
import math

import jax
import jax.numpy as jnp
from jax import lax
from jax.experimental import pallas as pl
from jax.experimental.pallas import tpu as pltpu
from jax.sharding import PartitionSpec as P

MESH_IDS = pl.DeviceIdType.MESH


def tap_exchange_kernel(nz, nx, nc, scale, x_ref, o_ref, r1, s1, r2, s2, r3, mine, local_sem, sems):
    me = lax.axis_index("ctx")
    sec = lax.axis_index("section")
    core = me % nc
    xi = (me // nc) % nx
    zi = me // (nc * nx)

    def device(z, x, c):
        return (sec, (z * nx + x) * nc + c)

    peers = [device(zi, xi, 1 - core)]
    peers += [device(zi, (xi + k) % nx, core) for k in range(1, nx)]
    peers += [device((zi + k) % nz, xi, core) for k in range(1, nz)]
    barrier = pltpu.get_barrier_semaphore()
    for peer in peers:
        pl.semaphore_signal(barrier, inc=1, device_id=peer, device_id_type=MESH_IDS)
    pl.semaphore_wait(barrier, len(peers))

    def send(src, dst, peer, out_slot, in_slot):
        return pltpu.make_async_remote_copy(
            src_ref=src,
            dst_ref=dst,
            send_sem=sems.at[0, out_slot],
            recv_sem=sems.at[1, in_slot],
            device_id=peer,
            device_id_type=MESH_IDS,
        )

    first = send(x_ref.at[:, :, 1 - core], r1, peers[0], 0, 0)
    first.start()
    local = pltpu.make_async_copy(x_ref.at[:, :, core], mine, local_sem)
    local.start()
    local.wait()
    first.wait()
    s1[...] = mine[...] + r1[...]

    second = []
    for k in range(1, nx):
        target = (xi + k) % nx
        copy = send(s1.at[:, target], r2.at[xi], device(zi, target, core), 1 + target, 1 + xi)
        copy.start()
        second.append(copy)
    for k in range(1, nx):
        source = (xi + nx - k) % nx
        send(s1.at[:, source], r2.at[source], device(zi, source, core), 1 + source, 1 + source).wait_recv()
    for copy in second:
        copy.wait_send()
    r2[xi] = s1[:, xi]
    s2[...] = jnp.sum(r2[...], axis=0)

    third = []
    for k in range(1, nz):
        target = (zi + k) % nz
        copy = send(s2.at[target], r3.at[zi], device(target, xi, core), 1 + nx + target, 1 + nx + zi)
        copy.start()
        third.append(copy)
    for k in range(1, nz):
        source = (zi + nz - k) % nz
        send(s2.at[source], r3.at[source], device(source, xi, core), 1 + nx + source, 1 + nx + source).wait_recv()
    for copy in third:
        copy.wait_send()
    r3[zi] = s2[zi]
    o_ref[...] = (jnp.sum(r3[...], axis=0) * scale).astype(o_ref.dtype)


def tap_exchange(parts, scale):
    nz, nx, nc, taps, width = parts.shape
    return pl.pallas_call(
        functools.partial(tap_exchange_kernel, nz, nx, nc, scale),
        out_shape=jax.ShapeDtypeStruct((taps, width), jnp.bfloat16),
        in_specs=[pl.BlockSpec(memory_space=pl.ANY)],
        out_specs=pl.BlockSpec(memory_space=pltpu.VMEM),
        scratch_shapes=[
            pltpu.VMEM((nz, nx, taps, width), jnp.float32),
            pltpu.VMEM((nz, nx, taps, width), jnp.float32),
            pltpu.VMEM((nx, nz, taps, width), jnp.float32),
            pltpu.VMEM((nz, taps, width), jnp.float32),
            pltpu.VMEM((nz, taps, width), jnp.float32),
            pltpu.VMEM((nz, nx, taps, width), jnp.float32),
            pltpu.SemaphoreType.DMA(()),
            pltpu.SemaphoreType.DMA((2, 1 + nx + nz)),
        ],
        compiler_params=pltpu.CompilerParams(collective_id=0, has_side_effects=True),
    )(parts)


def channel_kernel(n, x_ref, o_ref, stage, local_sems, send_sems, recv_sems):
    count, channels, tokens = stage.shape
    rows = channels // n
    me = lax.axis_index("ctx")
    sec = lax.axis_index("section")
    barrier = pltpu.get_barrier_semaphore()

    def greet(k, carry):
        peer = lax.rem(me + k, n)
        pl.semaphore_signal(barrier, inc=1, device_id=(sec, peer), device_id_type=MESH_IDS)
        return carry

    lax.fori_loop(1, n, greet, 0)
    pl.semaphore_wait(barrier, n - 1)

    def copy(index, peer, source):
        return pltpu.make_async_remote_copy(
            src_ref=stage.at[index, pl.ds(pl.multiple_of(peer * rows, rows), rows), :],
            dst_ref=o_ref.at[index, :, pl.ds(pl.multiple_of(source * tokens, tokens), tokens)],
            send_sem=send_sems.at[index, peer],
            recv_sem=recv_sems.at[index, source],
            device_id=(sec, peer),
            device_id_type=MESH_IDS,
        )

    owns = []
    for index in range(count):
        stage[index] = x_ref[index].astype(jnp.float32).T.astype(stage.dtype)

        def start(k, carry, index=index):
            copy(index, lax.rem(me + k, n), me).start()
            return carry

        lax.fori_loop(1, n, start, 0)
        own = pltpu.make_async_copy(
            stage.at[index, pl.ds(pl.multiple_of(me * rows, rows), rows), :],
            o_ref.at[index, :, pl.ds(pl.multiple_of(me * tokens, tokens), tokens)],
            local_sems.at[index],
        )
        own.start()
        owns.append(own)

    for index in range(count):

        def finish(k, carry, index=index):
            source = lax.rem(me + n - k, n)
            copy(index, source, source).wait_recv()
            copy(index, lax.rem(me + k, n), me).wait_send()
            return carry

        lax.fori_loop(1, n, finish, 0)
        owns[index].wait()


def to_channels(x):
    n = lax.axis_size("ctx")
    count, tokens, channels = x.shape
    return pl.pallas_call(
        functools.partial(channel_kernel, n),
        out_shape=jax.ShapeDtypeStruct((count, channels // n, tokens * n), x.dtype),
        in_specs=[pl.BlockSpec(memory_space=pltpu.VMEM)],
        out_specs=pl.BlockSpec(memory_space=pltpu.VMEM),
        scratch_shapes=[
            pltpu.VMEM((count, channels, tokens), x.dtype),
            pltpu.SemaphoreType.DMA((count,)),
            pltpu.SemaphoreType.DMA((count, n)),
            pltpu.SemaphoreType.DMA((count, n)),
        ],
        compiler_params=pltpu.CompilerParams(collective_id=1, has_side_effects=True),
    )(x)


def passed_along(value, axis, steps):
    count = lax.axis_size(axis)
    pairs = [(source, (source + steps) % count) for source in range(count)]
    return lax.ppermute(value, axis, pairs)


def shifted(array, axis, by):
    devices = lax.axis_size(axis)
    pairs = [(i, i + by) for i in range(devices) if 0 <= i + by < devices]
    return lax.ppermute(array, axis, pairs)


def unit_roots(rows, cols, period):
    row_ids = jnp.arange(rows, dtype=jnp.int32)[:, None]
    col_ids = jnp.arange(cols, dtype=jnp.int32)[None, :]
    angle = (row_ids * col_ids % period).astype(jnp.float32) * (-2.0 * math.pi / period)
    return (jnp.cos(angle), jnp.sin(angle))


def contract(form, left, right):
    return jnp.einsum(
        form, left, right, precision=lax.Precision.HIGH, preferred_element_type=jnp.float32
    )


def to_spectrum(parts, factor_a, factor_b):
    channels = parts.shape[0]
    inputs_count = parts.shape[1]
    half = factor_a // 2
    period = factor_a * factor_b
    fa_cos, fa_sin = unit_roots(factor_a, half, factor_a)
    first_table = jnp.stack([jnp.stack([fa_cos, -fa_sin]), jnp.stack([fa_sin, fa_cos])])[
        :, :inputs_count
    ]
    tw_cos, tw_sin = unit_roots(factor_a, factor_b, period)
    fb_cos, fb_sin = unit_roots(factor_b, factor_b, factor_b)
    second_table = jnp.stack([jnp.stack([fb_cos, fb_sin]), jnp.stack([-fb_sin, fb_cos])])
    shaped = parts.reshape(channels, inputs_count, half, factor_b)
    first = contract("qrca,nrab->nqcb", first_table, shaped)
    first_re = first[:, 0]
    first_im = first[:, 1]
    turned = jnp.stack(
        [first_re * tw_cos - first_im * tw_sin, first_re * tw_sin + first_im * tw_cos], 1
    )
    return contract("nqcb,qpbd->npcd", turned, second_table)


def from_spectrum(spectrum, factor_a, factor_b, scale):
    channels = spectrum.shape[0]
    half = factor_a // 2
    period = factor_a * factor_b
    fb_cos, fb_sin = unit_roots(factor_b, factor_b, factor_b)
    back_table = jnp.stack([jnp.stack([fb_cos, -fb_sin]), jnp.stack([fb_sin, fb_cos])])
    tw_cos, tw_sin = unit_roots(factor_a, factor_b, period)
    fa_cos, fa_sin = unit_roots(half, factor_a, factor_a)
    last_table = jnp.stack(
        [
            jnp.stack([fa_cos, fa_sin]) * (scale / period),
            jnp.stack([-fa_sin, fa_cos]) * (1.0 / period),
        ]
    )
    middle = contract("npcd,pqdb->nqcb", spectrum, back_table)
    middle_re = middle[:, 0]
    middle_im = middle[:, 1]
    turned = jnp.stack(
        [middle_re * tw_cos + middle_im * tw_sin, middle_im * tw_cos - middle_re * tw_sin], 1
    )
    result = contract("rqac,nqcb->nrab", last_table, turned)
    length = half * factor_b
    return (result[:, 0].reshape(channels, length), result[:, 1].reshape(channels, length))


def depthwise(extended, kernel):
    result = lax.conv_general_dilated(
        extended[None],
        kernel[:, None, :],
        (1,),
        "VALID",
        dimension_numbers=("NWC", "WIO", "NWC"),
        feature_group_count=extended.shape[1],
        preferred_element_type=jnp.float32,
    )
    return result[0]


def per_device(
    incoming, layer_input, pre_gate, mid_gate, long_gate, out_gate, long_filter, mid_filter
):
    sections = lax.axis_size("section")
    beta = (2.0 * sections) ** (-0.5)
    adjoint = passed_along(incoming[0], "section", -1).astype(jnp.float32)
    inputs = layer_input[0].astype(jnp.float32)
    tokens = inputs.shape[0]
    gate_pre = pre_gate[0].astype(jnp.float32)
    gate_mid = mid_gate[0].astype(jnp.float32)
    gate_long = long_gate[0].astype(jnp.float32)
    gate_out = out_gate[0].astype(jnp.float32)
    filter_taps = mid_filter[0]
    reach = filter_taps.shape[0] - 1
    seq_len = tokens * lax.axis_size("ctx")
    scale = float(seq_len) ** (-0.5)
    mixed_in = (inputs * gate_pre).astype(jnp.bfloat16)
    earlier = shifted(mixed_in[tokens - reach :], "ctx", 1)
    extended = jnp.concatenate([earlier, mixed_in], 0)
    flip = jnp.eye(filter_taps.shape[0], dtype=filter_taps.dtype)[::-1]
    flipped_taps = jnp.dot(flip, filter_taps, preferred_element_type=jnp.float32)
    branch = depthwise(extended, flipped_taps.astype(filter_taps.dtype))
    resid = inputs + beta * branch * gate_mid
    long_in = (resid * gate_long).astype(jnp.bfloat16)
    grad_z = (beta * adjoint * gate_out).astype(jnp.bfloat16)
    channel_z, channel_w = to_channels(jnp.stack([grad_z, long_in]))
    factor_b = math.gcd(seq_len, 128)
    factor_a = 2 * seq_len // factor_b
    zspec = to_spectrum(channel_z[:, None], factor_a, factor_b)
    zspec_re = zspec[:, 0]
    zspec_im = zspec[:, 1]
    pair = to_spectrum(jnp.stack([channel_w, -long_filter[0]], 1), factor_a, factor_b)
    pair_re = pair[:, 0]
    pair_im = pair[:, 1]
    joint_re = zspec_re * pair_re + zspec_im * pair_im
    joint_im = zspec_im * pair_re - zspec_re * pair_im
    lag_grad, input_part = from_spectrum(
        jnp.stack([joint_re, joint_im], 1), factor_a, factor_b, scale
    )
    long_grad = lag_grad.astype(jnp.bfloat16)[None]
    returned = lax.all_to_all(
        input_part.astype(jnp.bfloat16), "ctx", split_axis=1, concat_axis=0, tiled=True
    ).T
    grad_u = adjoint + returned.astype(jnp.float32) * gate_long
    grad_b = (beta * grad_u * gate_mid).astype(jnp.bfloat16)
    later = shifted(grad_b[:reach], "ctx", -1)
    grad_act = depthwise(jnp.concatenate([grad_b, later], 0), filter_taps)
    input_grad = (grad_u + grad_act * gate_pre).astype(jnp.bfloat16)[None]
    tap_part = lax.conv_general_dilated(
        extended[None],
        grad_b[:, None, :],
        (1,),
        "VALID",
        dimension_numbers=("NWC", "WIO", "NCW"),
        feature_group_count=extended.shape[1],
        preferred_element_type=jnp.float32,
    )[0]
    devices = lax.axis_size("ctx")
    columns = tap_part.shape[0] // devices
    chip_cores, chips_x = 2, 4
    chips_z = devices // (chip_cores * chips_x)
    parts = tap_part.reshape(chips_z, chips_x, chip_cores, columns, tap_part.shape[1])
    summed = tap_exchange(parts, scale)
    taps_flip = jnp.eye(summed.shape[1], dtype=summed.dtype)[::-1]
    mid_grad = jnp.dot(summed, taps_flip, preferred_element_type=jnp.float32)
    mid_grad = mid_grad.astype(summed.dtype).T[None]
    return (input_grad, long_grad, mid_grad)


def solution(mesh):
    placed = (
        P("section", "ctx", None),
        P("section", "ctx", None),
        P("section", "ctx", None),
        P("section", "ctx", None),
        P("section", "ctx", None),
        P("section", "ctx", None),
        P("section", "ctx", None),
        P("section", None, None),
    )
    return jax.shard_map(
        per_device,
        mesh=mesh,
        in_specs=placed,
        out_specs=(P("section", "ctx", None), P("section", "ctx", None), P("section", None, "ctx")),
        check_vma=False,
    )
```

```python
import functools
import math

import jax
import jax.numpy as jnp
from jax import lax
from jax.experimental import pallas as pl
from jax.experimental.pallas import tpu as pltpu
from jax.sharding import PartitionSpec as P

MESH_IDS = pl.DeviceIdType.MESH


def tap_exchange_kernel(nz, nx, nc, scale, x_ref, o_ref, r1, s1, r2, s2, r3, mine, local_sem, sems):
    me = lax.axis_index("ctx")
    sec = lax.axis_index("section")
    core = me % nc
    xi = (me // nc) % nx
    zi = me // (nc * nx)

    def device(z, x, c):
        return (sec, (z * nx + x) * nc + c)

    peers = [device(zi, xi, 1 - core)]
    peers += [device(zi, (xi + k) % nx, core) for k in range(1, nx)]
    peers += [device((zi + k) % nz, xi, core) for k in range(1, nz)]
    barrier = pltpu.get_barrier_semaphore()
    for peer in peers:
        pl.semaphore_signal(barrier, inc=1, device_id=peer, device_id_type=MESH_IDS)
    pl.semaphore_wait(barrier, len(peers))

    def send(src, dst, peer, out_slot, in_slot):
        return pltpu.make_async_remote_copy(
            src_ref=src,
            dst_ref=dst,
            send_sem=sems.at[0, out_slot],
            recv_sem=sems.at[1, in_slot],
            device_id=peer,
            device_id_type=MESH_IDS,
        )

    first = send(x_ref.at[:, :, 1 - core], r1, peers[0], 0, 0)
    first.start()
    local = pltpu.make_async_copy(x_ref.at[:, :, core], mine, local_sem)
    local.start()
    local.wait()
    first.wait()
    s1[...] = mine[...] + r1[...]

    second = []
    for k in range(1, nx):
        target = (xi + k) % nx
        copy = send(s1.at[:, target], r2.at[xi], device(zi, target, core), 1 + target, 1 + xi)
        copy.start()
        second.append(copy)
    for k in range(1, nx):
        source = (xi + nx - k) % nx
        send(s1.at[:, source], r2.at[source], device(zi, source, core), 1 + source, 1 + source).wait_recv()
    for copy in second:
        copy.wait_send()
    r2[xi] = s1[:, xi]
    s2[...] = jnp.sum(r2[...], axis=0)

    third = []
    for k in range(1, nz):
        target = (zi + k) % nz
        copy = send(s2.at[target], r3.at[zi], device(target, xi, core), 1 + nx + target, 1 + nx + zi)
        copy.start()
        third.append(copy)
    for k in range(1, nz):
        source = (zi + nz - k) % nz
        send(s2.at[source], r3.at[source], device(source, xi, core), 1 + nx + source, 1 + nx + source).wait_recv()
    for copy in third:
        copy.wait_send()
    r3[zi] = s2[zi]
    o_ref[...] = (jnp.sum(r3[...], axis=0) * scale).astype(o_ref.dtype)


def tap_exchange(parts, scale):
    nz, nx, nc, taps, width = parts.shape
    return pl.pallas_call(
        functools.partial(tap_exchange_kernel, nz, nx, nc, scale),
        out_shape=jax.ShapeDtypeStruct((taps, width), jnp.bfloat16),
        in_specs=[pl.BlockSpec(memory_space=pl.ANY)],
        out_specs=pl.BlockSpec(memory_space=pltpu.VMEM),
        scratch_shapes=[
            pltpu.VMEM((nz, nx, taps, width), jnp.float32),
            pltpu.VMEM((nz, nx, taps, width), jnp.float32),
            pltpu.VMEM((nx, nz, taps, width), jnp.float32),
            pltpu.VMEM((nz, taps, width), jnp.float32),
            pltpu.VMEM((nz, taps, width), jnp.float32),
            pltpu.VMEM((nz, nx, taps, width), jnp.float32),
            pltpu.SemaphoreType.DMA(()),
            pltpu.SemaphoreType.DMA((2, 1 + nx + nz)),
        ],
        compiler_params=pltpu.CompilerParams(collective_id=0, has_side_effects=True),
    )(parts)


def channel_kernel(n, x_ref, o_ref, stage, local_sems, send_sems, recv_sems):
    count, channels, tokens = stage.shape
    rows = channels // n
    me = lax.axis_index("ctx")
    sec = lax.axis_index("section")
    barrier = pltpu.get_barrier_semaphore()

    def greet(k, carry):
        peer = lax.rem(me + k, n)
        pl.semaphore_signal(barrier, inc=1, device_id=(sec, peer), device_id_type=MESH_IDS)
        return carry

    lax.fori_loop(1, n, greet, 0)
    pl.semaphore_wait(barrier, n - 1)

    def copy(index, peer, source):
        return pltpu.make_async_remote_copy(
            src_ref=stage.at[index, pl.ds(pl.multiple_of(peer * rows, rows), rows), :],
            dst_ref=o_ref.at[index, :, pl.ds(pl.multiple_of(source * tokens, tokens), tokens)],
            send_sem=send_sems.at[index, peer],
            recv_sem=recv_sems.at[index, source],
            device_id=(sec, peer),
            device_id_type=MESH_IDS,
        )

    owns = []
    for index in range(count):
        stage[index] = x_ref[index].astype(jnp.float32).T.astype(stage.dtype)

        def start(k, carry, index=index):
            copy(index, lax.rem(me + k, n), me).start()
            return carry

        lax.fori_loop(1, n, start, 0)
        own = pltpu.make_async_copy(
            stage.at[index, pl.ds(pl.multiple_of(me * rows, rows), rows), :],
            o_ref.at[index, :, pl.ds(pl.multiple_of(me * tokens, tokens), tokens)],
            local_sems.at[index],
        )
        own.start()
        owns.append(own)

    for index in range(count):

        def finish(k, carry, index=index):
            source = lax.rem(me + n - k, n)
            copy(index, source, source).wait_recv()
            copy(index, lax.rem(me + k, n), me).wait_send()
            return carry

        lax.fori_loop(1, n, finish, 0)
        owns[index].wait()


def to_channels(x):
    n = lax.axis_size("ctx")
    count, tokens, channels = x.shape
    return pl.pallas_call(
        functools.partial(channel_kernel, n),
        out_shape=jax.ShapeDtypeStruct((count, channels // n, tokens * n), x.dtype),
        in_specs=[pl.BlockSpec(memory_space=pltpu.VMEM)],
        out_specs=pl.BlockSpec(memory_space=pl.ANY),
        scratch_shapes=[
            pltpu.VMEM((count, channels, tokens), x.dtype),
            pltpu.SemaphoreType.DMA((count,)),
            pltpu.SemaphoreType.DMA((count, n)),
            pltpu.SemaphoreType.DMA((count, n)),
        ],
        compiler_params=pltpu.CompilerParams(collective_id=1, has_side_effects=True),
    )(x)


def passed_along(value, axis, steps):
    count = lax.axis_size(axis)
    pairs = [(source, (source + steps) % count) for source in range(count)]
    return lax.ppermute(value, axis, pairs)


def shifted(array, axis, by):
    devices = lax.axis_size(axis)
    pairs = [(i, i + by) for i in range(devices) if 0 <= i + by < devices]
    return lax.ppermute(array, axis, pairs)


def unit_roots(rows, cols, period):
    row_ids = jnp.arange(rows, dtype=jnp.int32)[:, None]
    col_ids = jnp.arange(cols, dtype=jnp.int32)[None, :]
    angle = (row_ids * col_ids % period).astype(jnp.float32) * (-2.0 * math.pi / period)
    return (jnp.cos(angle), jnp.sin(angle))


def contract(form, left, right):
    return jnp.einsum(
        form, left, right, precision=lax.Precision.HIGH, preferred_element_type=jnp.float32
    )


def to_spectrum(parts, factor_a, factor_b):
    channels = parts.shape[0]
    inputs_count = parts.shape[1]
    half = factor_a // 2
    period = factor_a * factor_b
    fa_cos, fa_sin = unit_roots(factor_a, half, factor_a)
    first_table = jnp.stack([jnp.stack([fa_cos, -fa_sin]), jnp.stack([fa_sin, fa_cos])])[
        :, :inputs_count
    ]
    tw_cos, tw_sin = unit_roots(factor_a, factor_b, period)
    fb_cos, fb_sin = unit_roots(factor_b, factor_b, factor_b)
    second_table = jnp.stack([jnp.stack([fb_cos, fb_sin]), jnp.stack([-fb_sin, fb_cos])])
    shaped = parts.reshape(channels, inputs_count, half, factor_b)
    first = contract("qrca,nrab->nqcb", first_table, shaped)
    first_re = first[:, 0]
    first_im = first[:, 1]
    turned = jnp.stack(
        [first_re * tw_cos - first_im * tw_sin, first_re * tw_sin + first_im * tw_cos], 1
    )
    return contract("nqcb,qpbd->npcd", turned, second_table)


def from_spectrum(spectrum, factor_a, factor_b, scale):
    channels = spectrum.shape[0]
    half = factor_a // 2
    period = factor_a * factor_b
    fb_cos, fb_sin = unit_roots(factor_b, factor_b, factor_b)
    back_table = jnp.stack([jnp.stack([fb_cos, -fb_sin]), jnp.stack([fb_sin, fb_cos])])
    tw_cos, tw_sin = unit_roots(factor_a, factor_b, period)
    fa_cos, fa_sin = unit_roots(half, factor_a, factor_a)
    last_table = jnp.stack(
        [
            jnp.stack([fa_cos, fa_sin]) * (scale / period),
            jnp.stack([-fa_sin, fa_cos]) * (1.0 / period),
        ]
    )
    middle = contract("npcd,pqdb->nqcb", spectrum, back_table)
    middle_re = middle[:, 0]
    middle_im = middle[:, 1]
    turned = jnp.stack(
        [middle_re * tw_cos + middle_im * tw_sin, middle_im * tw_cos - middle_re * tw_sin], 1
    )
    result = contract("rqac,nqcb->nrab", last_table, turned)
    length = half * factor_b
    return (result[:, 0].reshape(channels, length), result[:, 1].reshape(channels, length))


def depthwise(extended, kernel):
    result = lax.conv_general_dilated(
        extended[None],
        kernel[:, None, :],
        (1,),
        "VALID",
        dimension_numbers=("NWC", "WIO", "NWC"),
        feature_group_count=extended.shape[1],
        preferred_element_type=jnp.float32,
    )
    return result[0]


def per_device(
    incoming, layer_input, pre_gate, mid_gate, long_gate, out_gate, long_filter, mid_filter
):
    sections = lax.axis_size("section")
    beta = (2.0 * sections) ** (-0.5)
    adjoint = passed_along(incoming[0], "section", -1).astype(jnp.float32)
    inputs = layer_input[0].astype(jnp.float32)
    tokens = inputs.shape[0]
    gate_pre = pre_gate[0].astype(jnp.float32)
    gate_mid = mid_gate[0].astype(jnp.float32)
    gate_long = long_gate[0].astype(jnp.float32)
    gate_out = out_gate[0].astype(jnp.float32)
    filter_taps = mid_filter[0]
    reach = filter_taps.shape[0] - 1
    seq_len = tokens * lax.axis_size("ctx")
    scale = float(seq_len) ** (-0.5)
    mixed_in = (inputs * gate_pre).astype(jnp.bfloat16)
    earlier = shifted(mixed_in[tokens - reach :], "ctx", 1)
    extended = jnp.concatenate([earlier, mixed_in], 0)
    flip = jnp.eye(filter_taps.shape[0], dtype=filter_taps.dtype)[::-1]
    flipped_taps = jnp.dot(flip, filter_taps, preferred_element_type=jnp.float32)
    branch = depthwise(extended, flipped_taps.astype(filter_taps.dtype))
    resid = inputs + beta * branch * gate_mid
    long_in = (resid * gate_long).astype(jnp.bfloat16)
    grad_z = (beta * adjoint * gate_out).astype(jnp.bfloat16)
    channel_z, channel_w = to_channels(jnp.stack([grad_z, long_in]))
    factor_b = math.gcd(seq_len, 128)
    factor_a = 2 * seq_len // factor_b
    zspec = to_spectrum(channel_z[:, None], factor_a, factor_b)
    zspec_re = zspec[:, 0]
    zspec_im = zspec[:, 1]
    pair = to_spectrum(jnp.stack([channel_w, -long_filter[0]], 1), factor_a, factor_b)
    pair_re = pair[:, 0]
    pair_im = pair[:, 1]
    joint_re = zspec_re * pair_re + zspec_im * pair_im
    joint_im = zspec_im * pair_re - zspec_re * pair_im
    lag_grad, input_part = from_spectrum(
        jnp.stack([joint_re, joint_im], 1), factor_a, factor_b, scale
    )
    long_grad = lag_grad.astype(jnp.bfloat16)[None]
    returned = lax.all_to_all(
        input_part.astype(jnp.bfloat16), "ctx", split_axis=1, concat_axis=0, tiled=True
    ).T
    grad_u = adjoint + returned.astype(jnp.float32) * gate_long
    grad_b = (beta * grad_u * gate_mid).astype(jnp.bfloat16)
    later = shifted(grad_b[:reach], "ctx", -1)
    grad_act = depthwise(jnp.concatenate([grad_b, later], 0), filter_taps)
    input_grad = (grad_u + grad_act * gate_pre).astype(jnp.bfloat16)[None]
    tap_part = lax.conv_general_dilated(
        extended[None],
        grad_b[:, None, :],
        (1,),
        "VALID",
        dimension_numbers=("NWC", "WIO", "NCW"),
        feature_group_count=extended.shape[1],
        preferred_element_type=jnp.float32,
    )[0]
    devices = lax.axis_size("ctx")
    columns = tap_part.shape[0] // devices
    chip_cores, chips_x = 2, 4
    chips_z = devices // (chip_cores * chips_x)
    parts = tap_part.reshape(chips_z, chips_x, chip_cores, columns, tap_part.shape[1])
    summed = tap_exchange(parts, scale)
    taps_flip = jnp.eye(summed.shape[1], dtype=summed.dtype)[::-1]
    mid_grad = jnp.dot(summed, taps_flip, preferred_element_type=jnp.float32)
    mid_grad = mid_grad.astype(summed.dtype).T[None]
    return (input_grad, long_grad, mid_grad)


def solution(mesh):
    placed = (
        P("section", "ctx", None),
        P("section", "ctx", None),
        P("section", "ctx", None),
        P("section", "ctx", None),
        P("section", "ctx", None),
        P("section", "ctx", None),
        P("section", "ctx", None),
        P("section", None, None),
    )
    return jax.shard_map(
        per_device,
        mesh=mesh,
        in_specs=placed,
        out_specs=(P("section", "ctx", None), P("section", "ctx", None), P("section", None, "ctx")),
        check_vma=False,
    )
```
